32 devices in a mesh: lon: 8 (over z, y), lat: 4 (over x, core).
Axes of the slice: x: 2, y: 2, z: 4, core: 2. Of those that a mesh axis runs over, the one named last changes fastest.
Arguments:
- surface_adjoint: float32 [1024, 8192], P('lat', 'lon'), may hold values from -6 to 6
- east_adjoint: float32 [1024, 8192], P('lat', 'lon'), may hold values from -6 to 6
- north_adjoint: float32 [1024, 8192], P('lat', 'lon'), may hold values from -6 to 6
- water_depth: float32 [1024, 8192], P('lat', 'lon'), may hold values from 0.3 to 1
- wet_mask: int32 [1024, 8192], P('lat', 'lon'), may hold values 0 or 1
- control_active: int32 [64, 512], P('lat', 'lon'), may hold values 0 or 1
Outputs:
- surface_after: float32 [1024, 8192], P('lat', 'lon')
- east_after: float32 [1024, 8192], P('lat', 'lon')
- north_after: float32 [1024, 8192], P('lat', 'lon')
- uplift_grad: float32 [64, 512], P('lat', 'lon')
The draws below stay inside these ranges and needn't reach their ends.
All inputs are finite; a program needn't handle non-finite values. No bound on the sum of `wet_mask` or of `control_active` on one device may be relied on, other than what follows from the above.
Results may differ from the reference program's by a relative error of at most 0.00021.
Values sent between devices are 32-bit elements; how exact they have to be, the bound alone decides.
No kernel may reach another device: no remote copies, remote signals or barrier semaphores. Data moves between devices by JAX's collectives and lax.ppermute only.
A program may use at most 64 MiB of HBM per device.

```python
import math
import jax
import jax.numpy as jnp
from jax import lax

SPACING = 16
STEPS = 3
NLAT = 1024
NLON = 8192
KALL = 64
KOLL = 512


def set_ends(drawn, stream_key, least, high):
    extent = drawn.shape
    spot = [jax.random.randint(jax.random.fold_in(stream_key, axis), (), 0, extent[axis]) for axis in range(len(extent))]
    drawn = drawn.at[tuple(spot)].set(least)
    longest = extent.index(max(extent))
    spot[longest] = (spot[longest] + 1) % extent[longest]
    return drawn.at[tuple(spot)].set(high)


def levels(key, dims, cuts, smallest, high):
    loudness = 1.0
    for dim, shards_of in cuts:
        heights = jax.random.uniform(jax.random.fold_in(jax.random.fold_in(key, 6), dim), (shards_of,), jnp.float32, smallest / len(cuts), high / len(cuts))
        loudness = loudness * jnp.repeat(jnp.exp(heights), dims[dim] // shards_of).reshape((-1,) + (1,) * (len(dims) - 1 - dim))
    return loudness


def noise(own_key, shape, deviation, bound, cuts=(), kind=jnp.bfloat16):
    gain = levels(own_key, shape, cuts, -0.22, 0.18) if cuts else 1.0
    result = jax.random.normal(own_key, shape, jnp.float32) * deviation * gain
    return jnp.minimum(jnp.maximum(result, -bound), bound).astype(kind)


def setup_inputs(seed: int = 0) -> dict:
    keys = jax.random.split(jax.random.key(seed), 7)
    surface_adjoint = noise(keys[0], (NLAT, NLON), 1.0, 6.0, ((0, 4), (1, 8)), jnp.float32)
    east_adjoint = noise(keys[1], (NLAT, NLON), 1.0, 6.0, ((0, 4), (1, 8)), jnp.float32)
    north_adjoint = noise(keys[2], (NLAT, NLON), 1.0, 6.0, ((0, 4), (1, 8)), jnp.float32)
    water_depth = jnp.clip(jnp.exp(math.log(1.0) - 1.2039728 * jax.random.uniform(keys[3], (NLAT, NLON), jnp.float32) ** levels(keys[3], (NLAT, NLON), ((0, 4), (1, 8)), -0.2, 0.2)), 0.3, 1.0)
    wet_mask = set_ends((jax.random.randint(keys[4], (NLAT, NLON), 0, 10) < 9).astype(jnp.int32), jax.random.fold_in(keys[4], 1), 0, 1)
    control_active = set_ends((jax.random.randint(keys[5], (KALL, KOLL), 0, 4) < 3).astype(jnp.int32), jax.random.fold_in(keys[5], 1), 0, 1)
    return dict(surface_adjoint=surface_adjoint, east_adjoint=east_adjoint, north_adjoint=north_adjoint, water_depth=water_depth, wet_mask=wet_mask, control_active=control_active)


courant = 0.5


def from_east(field):
    return jnp.pad(field[:, 1:], ((0, 0), (0, 1)))


def west_incoming(field):
    return jnp.pad(field[:, :-1], ((0, 0), (1, 0)))


def from_north(field):
    return jnp.pad(field[1:, :], ((0, 1), (0, 0)))


def from_south(field):
    return jnp.pad(field[:-1, :], ((1, 0), (0, 0)))


def march_steps(surface_height, eastward, northward, wet_depth, wet_fraction):
    for step in range(STEPS):
        eastward = wet_fraction * (eastward + courant * wet_depth * (from_east(surface_height) - west_incoming(surface_height)))
        northward = wet_fraction * (northward + courant * wet_depth * (from_north(surface_height) - from_south(surface_height)))
        surface_height = wet_fraction * (surface_height + courant * ((from_east(eastward) - west_incoming(eastward)) + (from_north(northward) - from_south(northward))))
    return surface_height, eastward, northward


def spline_weight(arg):
    mag = jnp.abs(arg)
    inner = 2.0 / 3.0 - mag * mag + 0.5 * mag * mag * mag
    outer = (2.0 - mag) * (2.0 - mag) * (2.0 - mag) / 6.0
    return jnp.where(mag < 1.0, inner, jnp.where(mag < 2.0, outer, 0.0 * mag))


def move_rows(block, offset):
    if offset > 0:
        return jnp.pad(block, ((offset, 0), (0, 0)))[:-offset]
    if offset < 0:
        return jnp.pad(block, ((0, -offset), (0, 0)))[-offset:]
    return block


def reference(surface_adjoint, east_adjoint, north_adjoint, water_depth, wet_mask, control_active):
    wet_fraction = wet_mask.astype(jnp.float32)
    wet_depth = water_depth * wet_fraction
    surface_height, eastward, northward = march_steps(surface_adjoint, east_adjoint, north_adjoint, wet_depth, wet_fraction)
    lag = (jnp.arange(5, dtype=jnp.float32) - 2.0)[:, None]
    inside = (jnp.arange(SPACING, dtype=jnp.float32)[None, :] + 0.5) / SPACING
    weight_table = spline_weight(inside - 0.5 - lag)

    def band(block):
        cubic_basis = block.reshape(SPACING, KOLL, SPACING)
        half_width = jnp.einsum('lq,qgw->lgw', weight_table, cubic_basis, precision=lax.Precision.HIGHEST)
        return jnp.einsum('dbr,er->dbe', half_width, weight_table, precision=lax.Precision.HIGHEST)

    parts = lax.map(band, surface_height.reshape(KALL, SPACING, NLON))
    sums = jnp.zeros((KALL, KOLL), jnp.float32)
    for lag_row in range(5):
        for lag_col in range(5):
            piece = move_rows(parts[:, lag_row, :, lag_col], lag_row - 2)
            piece = move_rows(piece.T, lag_col - 2).T
            sums = sums + piece
    uplift_grad = sums * control_active.astype(jnp.float32) / SPACING
    return surface_height, eastward, northward, uplift_grad
```

```python
import functools

import jax
import jax.numpy as jnp
from jax import lax
from jax.experimental import pallas as pl
from jax.experimental.pallas import tpu as pltpu
from jax.sharding import PartitionSpec as P

SPACING = 16
STEPS = 3
COURANT = 0.5
LANES = 128
SUB = 8
HALO = 32
EDGE = 2 * STEPS
STRIP = HALO + 16
CHUNK = 64
F32 = jnp.float32
ANY = pl.BlockSpec(memory_space=pl.ANY)
VMEM = pl.BlockSpec(memory_space=pltpu.VMEM)


def lane_index():
    return lax.broadcasted_iota(jnp.int32, (SUB, LANES), 1)


def east_minus_west(tiles):
    n = len(tiles)
    up = [pltpu.roll(t, LANES - 1, 1) for t in tiles]
    down = [pltpu.roll(t, 1, 1) for t in tiles]
    if n == 1:
        return [up[0] - down[0]]
    lane = lane_index()
    return [
        jnp.where(lane == LANES - 1, up[(c + 1) % n], up[c])
        - jnp.where(lane == 0, down[(c - 1) % n], down[c])
        for c in range(n)
    ]


def rows_at(ref, c, r):
    return ref[c, pl.ds(r, SUB), :]


def flux_rows(refs, r, tiles):
    S, E, N, Q, W = refs
    ds = east_minus_west([rows_at(S, c, r) for c in range(tiles)])
    for c in range(tiles):
        q = rows_at(Q, c, r)
        E[c, pl.ds(r, SUB), :] = rows_at(E, c, r) + q * ds[c]
        N[c, pl.ds(r, SUB), :] = rows_at(N, c, r) + q * (rows_at(S, c, r + 1) - rows_at(S, c, r - 1))


def surface_rows(refs, r, tiles, first):
    S, E, N, Q, W = refs
    de = east_minus_west([rows_at(E, c, r) for c in range(tiles)])
    for c in range(tiles):
        hw = rows_at(W, c, r)
        s = rows_at(S, c, r)
        if first:
            s = s * (hw + hw)
        S[c, pl.ds(r, SUB), :] = s + hw * (de[c] + (rows_at(N, c, r + 1) - rows_at(N, c, r - 1)))


def loop_rows(count, body, unroll=8):
    while count % unroll:
        unroll -= 1

    def step(i, carry):
        base = pl.multiple_of(i * (unroll * SUB), unroll * SUB) + SUB
        for u in range(unroll):
            body(base + u * SUB)
        return carry

    lax.fori_loop(0, count // unroll, step, 0)


def spline_weight(arg):
    mag = jnp.abs(arg)
    inner = 2.0 / 3.0 - mag * mag + 0.5 * mag * mag * mag
    outer = (2.0 - mag) * (2.0 - mag) * (2.0 - mag) / 6.0
    return jnp.where(mag < 1.0, inner, jnp.where(mag < 2.0, outer, 0.0 * mag))


def spline_of(cell, point):
    return spline_weight((cell.astype(F32) + 0.5) / SPACING - (point.astype(F32) + 0.5))


def dot(a, b):
    return jnp.dot(a, b, precision=lax.Precision.HIGHEST, preferred_element_type=F32)


def zero_borders(refs, rows, tiles):
    z = jnp.zeros((SUB, LANES), F32)
    for ref in refs:
        for c in range(tiles):
            ref[c, 0:SUB, :] = z
            ref[c, SUB + rows : SUB + rows + SUB, :] = z


def wait_all(copies):
    for copy in copies:
        copy.wait()


def is_even(axis):
    return lax.rem(lax.axis_index(axis), 2) == 0


def pack_rows_kernel(s, e, n, d, m, pa, pb, depth, mask, sem):
    rows = s.shape[0]
    even = is_even("lat")
    top = rows - HALO
    starts = (jnp.where(even, top, 0), jnp.where(even, 0, top))
    copies = []
    for side, (out, row) in enumerate(zip((pa, pb), starts)):
        at = pl.ds(pl.multiple_of(row, SUB), HALO)
        for f, (src, dst) in enumerate(
            (
                (s, out.at[0:HALO]),
                (e, out.at[HALO : 2 * HALO]),
                (n, out.at[2 * HALO : 3 * HALO]),
                (d, depth.at[side]),
                (m, mask.at[side]),
            )
        ):
            copy = pltpu.make_async_copy(src.at[at, :], dst, sem.at[side, f])
            copy.start()
            copies.append(copy)
    wait_all(copies)
    for side, out in enumerate((pa, pb)):
        wet = mask[side].astype(F32)
        out[HALO : 2 * HALO] = out[HALO : 2 * HALO] * wet
        out[2 * HALO : 3 * HALO] = out[2 * HALO : 3 * HALO] * wet
        out[3 * HALO : 4 * HALO] = depth[side] * (COURANT * wet)


def pack_rows(s, e, n, d, m):
    rows, cols = s.shape
    return pl.pallas_call(
        pack_rows_kernel,
        out_shape=[jax.ShapeDtypeStruct((4 * HALO, cols), F32)] * 2,
        in_specs=[ANY] * 5,
        out_specs=[VMEM] * 2,
        scratch_shapes=[
            pltpu.VMEM((2, HALO, cols), F32),
            pltpu.VMEM((2, HALO, cols), jnp.int32),
            pltpu.SemaphoreType.DMA((2, 5)),
        ],
        name="pack_rows",
    )(s, e, n, d, m)


def own_columns(first, last):
    lane = lane_index()
    both = jnp.where(lane < HALO, first, pltpu.roll(last, LANES // 2, 1))
    return jnp.where(lane < 2 * HALO, both, 0.0)


def pack_columns(own, even):
    group = lax.div(lane_index(), HALO)
    shift = jnp.where(even, 1, 0)
    pc = pd = None
    for f, tile in enumerate(own):
        turn = (f + 2) % 4
        moved = pltpu.roll(tile, turn * HALO, 1) if turn else tile
        if pc is None:
            pc = pd = moved
        else:
            pc = jnp.where(group == lax.rem(turn + shift, 4), moved, pc)
            pd = jnp.where(group == lax.rem(turn + 1 - shift, 4), moved, pd)
    return pc, pd


def interior_kernel(
    s, e, n, d, m, so, eo, no, u, pc, pd, own, S, E, N, Q, W, M, PC, PD, OWN, isem, osem, psem
):
    rows, cols = s.shape
    tiles = cols // LANES
    chunks = rows // CHUNK
    refs = (S, E, N, Q, W)
    even = is_even("lon")
    loads = []
    for k in range(chunks):
        copies = []
        for src, dst in ((s, S), (d, Q), (m, M), (e, E), (n, N)):
            for c in range(tiles):
                copy = pltpu.make_async_copy(
                    src.at[k * CHUNK : (k + 1) * CHUNK, c * LANES : (c + 1) * LANES],
                    dst.at[c, SUB + k * CHUNK : SUB + (k + 1) * CHUNK, :],
                    isem.at[k],
                )
                copy.start()
                copies.append(copy)
        loads.append(copies)
    zero_borders((S, N), rows, tiles)

    def first_flux(r):
        ds = east_minus_west([rows_at(S, c, r) for c in range(tiles)])
        ends = {}
        for c in range(tiles):
            wet = rows_at(M, c, r).astype(F32)
            hw = COURANT * wet
            q = rows_at(Q, c, r) * hw
            e0 = rows_at(E, c, r) * wet
            n0 = rows_at(N, c, r) * wet
            if c in (0, tiles - 1):
                ends[c] = (rows_at(S, c, r), e0, n0, q)
            W[c, pl.ds(r, SUB), :] = hw
            Q[c, pl.ds(r, SUB), :] = q
            E[c, pl.ds(r, SUB), :] = e0 + q * ds[c]
            N[c, pl.ds(r, SUB), :] = n0 + q * (rows_at(S, c, r + 1) - rows_at(S, c, r - 1))
        mine = [own_columns(a, b) for a, b in zip(ends[0], ends[tiles - 1])]
        for f in range(4):
            OWN[f, pl.ds(r - SUB, SUB), :] = mine[f]
        tc, td = pack_columns(mine, even)
        PC[pl.ds(r - SUB, SUB), :] = tc
        PD[pl.ds(r - SUB, SUB), :] = td

    def over_chunk(k, body):
        def shifted(r):
            body(r + k * CHUNK)

        loop_rows(CHUNK // SUB, shifted)

    wait_all(loads[0])
    for k in range(chunks):
        if k + 1 < chunks:
            wait_all(loads[k + 1])
        over_chunk(k, first_flux)
    sends = [
        pltpu.make_async_copy(PC, pc.at[HALO : HALO + rows], psem.at[0]),
        pltpu.make_async_copy(PD, pd.at[HALO : HALO + rows], psem.at[1]),
        pltpu.make_async_copy(OWN, own.at[:, HALO : HALO + rows], psem.at[2]),
    ]
    for copy in sends:
        copy.start()
    loop_rows(rows // SUB, lambda r: surface_rows(refs, r, tiles, True))
    for step in range(1, STEPS):
        last = step == STEPS - 1
        for k in range(chunks):
            over_chunk(k, lambda r: flux_rows(refs, r, tiles))
            if last:
                sends += store_rows(((E, eo), (N, no)), k, tiles, osem)
        for k in range(chunks):
            over_chunk(k, lambda r: surface_rows(refs, r, tiles, False))
            if last:
                sends += store_rows(((S, so),), k, tiles, osem)
    points = rows // SPACING
    cell = lax.broadcasted_iota(jnp.int32, (points, rows), 1)
    table = spline_of(cell, lax.broadcasted_iota(jnp.int32, (points, rows), 0))
    table = jnp.where((cell >= EDGE) & (cell < rows - EDGE), table, 0.0)
    for c in range(tiles):
        u[:, c * LANES : (c + 1) * LANES] = dot(table, S[c, SUB : SUB + rows, :])
    wait_all(sends)


def store_rows(pairs, k, tiles, sem):
    copies = []
    for src, dst in pairs:
        for c in range(tiles):
            copy = pltpu.make_async_copy(
                src.at[c, SUB + k * CHUNK : SUB + (k + 1) * CHUNK, :],
                dst.at[k * CHUNK : (k + 1) * CHUNK, c * LANES : (c + 1) * LANES],
                sem.at[0],
            )
            copy.start()
            copies.append(copy)
    return copies


def interior(s, e, n, d, m):
    rows, cols = s.shape
    tiles = cols // LANES
    field = jax.ShapeDtypeStruct((rows, cols), F32)
    wide = jax.ShapeDtypeStruct((rows + 2 * HALO, LANES), F32)
    return pl.pallas_call(
        interior_kernel,
        out_shape=[field] * 3
        + [
            jax.ShapeDtypeStruct((rows // SPACING, cols), F32),
            wide,
            wide,
            jax.ShapeDtypeStruct((4, rows + 2 * HALO, LANES), F32),
        ],
        in_specs=[ANY] * 5,
        out_specs=[ANY] * 3 + [VMEM] + [ANY] * 3,
        scratch_shapes=[pltpu.VMEM((tiles, rows + 2 * SUB, LANES), F32)] * 5
        + [
            pltpu.VMEM((tiles, rows + 2 * SUB, LANES), jnp.int32),
            pltpu.VMEM((rows, LANES), F32),
            pltpu.VMEM((rows, LANES), F32),
            pltpu.VMEM((4, rows, LANES), F32),
            pltpu.SemaphoreType.DMA((rows // CHUNK,)),
            pltpu.SemaphoreType.DMA((1,)),
            pltpu.SemaphoreType.DMA((3,)),
        ],
        cost_estimate=pl.CostEstimate(flops=40 * rows * cols, bytes_accessed=32 * rows * cols, transcendentals=0),
        name="interior",
    )(s, e, n, d, m)


def corner_kernel(ra, rb, pc_in, pd_in, own_in, pc, pd, own, X, PC, PD, OWN, sem, psem):
    del pc_in, pd_in, own_in
    height = pc.shape[0]
    cols = ra.shape[1]
    even, lon_even = is_even("lat"), is_even("lon")
    copies = []
    for side, src in enumerate((ra, rb)):
        for end, col in enumerate((0, cols - LANES)):
            copy = pltpu.make_async_copy(src.at[:, col : col + LANES], X.at[side, end], sem.at[side, end])
            copy.start()
            copies.append(copy)
    wait_all(copies)
    top = height - HALO
    starts = (jnp.where(even, top, 0), jnp.where(even, 0, top))
    sends = []
    for side, row in enumerate(starts):
        for r in range(0, HALO, SUB):
            mine = [
                own_columns(X[side, 0, f * HALO + r : f * HALO + r + SUB, :], X[side, 1, f * HALO + r : f * HALO + r + SUB, :])
                for f in range(4)
            ]
            for f in range(4):
                OWN[side, f, r : r + SUB, :] = mine[f]
            tc, td = pack_columns(mine, lon_even)
            PC[side, r : r + SUB, :] = tc
            PD[side, r : r + SUB, :] = td
        at = pl.ds(pl.multiple_of(row, SUB), HALO)
        for f, (src, dst) in enumerate(
            ((PC.at[side], pc.at[at, :]), (PD.at[side], pd.at[at, :]), (OWN.at[side], own.at[:, at, :]))
        ):
            copy = pltpu.make_async_copy(src, dst, psem.at[side, f])
            copy.start()
            sends.append(copy)
    wait_all(sends)


def corners(ra, rb, pc, pd, own):
    return pl.pallas_call(
        corner_kernel,
        out_shape=[jax.ShapeDtypeStruct(x.shape, F32) for x in (pc, pd, own)],
        in_specs=[ANY] * 5,
        out_specs=[ANY] * 3,
        scratch_shapes=[
            pltpu.VMEM((2, 2, 4 * HALO, LANES), F32),
            pltpu.VMEM((2, HALO, LANES), F32),
            pltpu.VMEM((2, HALO, LANES), F32),
            pltpu.VMEM((2, 4, HALO, LANES), F32),
            pltpu.SemaphoreType.DMA((2, 2)),
            pltpu.SemaphoreType.DMA((2, 3)),
        ],
        input_output_aliases={2: 0, 3: 1, 4: 2},
        name="corners",
    )(ra, rb, pc, pd, own)


def strip_kernel(s, e, n, d, m, ra, rb, u, so_in, eo_in, no_in, so, eo, no, v, S, E, N, Q, W, M, sem, osem):
    del so_in, eo_in, no_in
    rows, cols = s.shape
    tiles = cols // LANES
    refs = (S, E, N, Q, W)
    even = is_even("lat")
    keep = STRIP - HALO
    count = 2 * STRIP
    loads = []
    for src, dst in ((s, S), (e, E), (n, N), (d, Q), (m, M)):
        for row, to in ((0, HALO), (rows - keep, STRIP)):
            for c in range(tiles):
                copy = pltpu.make_async_copy(
                    src.at[row : row + keep, c * LANES : (c + 1) * LANES],
                    dst.at[c, SUB + to : SUB + to + keep, :],
                    sem.at[0],
                )
                copy.start()
                loads.append(copy)
    high = SUB + STRIP + keep
    for src, to in ((ra, jnp.where(even, high, SUB)), (rb, jnp.where(even, SUB, high))):
        at = pl.ds(pl.multiple_of(to, SUB), HALO)
        for f, dst in enumerate((S, E, N, Q)):
            for c in range(tiles):
                copy = pltpu.make_async_copy(
                    src.at[f * HALO : (f + 1) * HALO, c * LANES : (c + 1) * LANES],
                    dst.at[c, at, :],
                    sem.at[0],
                )
                copy.start()
                loads.append(copy)
    zero_borders((S, N), count, tiles)
    wait_all(loads)
    for c in range(tiles):
        for r in range(SUB + HALO, SUB + HALO + 2 * keep, SUB):
            wet = M[c, r : r + SUB, :].astype(F32)
            hw = COURANT * wet
            W[c, r : r + SUB, :] = hw
            Q[c, r : r + SUB, :] = Q[c, r : r + SUB, :] * hw
            E[c, r : r + SUB, :] = E[c, r : r + SUB, :] * wet
            N[c, r : r + SUB, :] = N[c, r : r + SUB, :] * wet
        for first in (SUB, high):
            for r in range(first, first + HALO, SUB):
                W[c, r : r + SUB, :] = jnp.where(Q[c, r : r + SUB, :] > 0.0, COURANT, 0.0)
    for step in range(STEPS):
        loop_rows(count // SUB, lambda r: flux_rows(refs, r, tiles), 12)
        loop_rows(count // SUB, lambda r: surface_rows(refs, r, tiles, step == 0), 12)
    sends = []
    for src, dst in ((S, so), (E, eo), (N, no)):
        for frm, to in ((SUB + HALO, 0), (SUB + STRIP + keep - SUB, rows - SUB)):
            for c in range(tiles):
                copy = pltpu.make_async_copy(
                    src.at[c, frm : frm + SUB, :],
                    dst.at[to : to + SUB, c * LANES : (c + 1) * LANES],
                    osem.at[0],
                )
                copy.start()
                sends.append(copy)
    points = rows // SPACING
    index = lax.broadcasted_iota(jnp.int32, (points, count), 1)
    cell = jnp.where(index < STRIP, index - HALO, index + (rows - keep - STRIP))
    table = spline_of(cell, lax.broadcasted_iota(jnp.int32, (points, count), 0))
    table = jnp.where((cell < EDGE) | (cell >= rows - EDGE), table, 0.0)
    across = cols // SPACING
    total = jnp.zeros((points, across), F32)
    for c in range(tiles):
        part = u[:, c * LANES : (c + 1) * LANES] + dot(table, S[c, SUB : SUB + count, :])
        col = lax.broadcasted_iota(jnp.int32, (LANES, across), 0) + c * LANES
        weights = spline_of(col, lax.broadcasted_iota(jnp.int32, (LANES, across), 1))
        weights = jnp.where((col >= EDGE) & (col < cols - EDGE), weights, 0.0)
        total = total + dot(part, weights)
    v[...] = total
    wait_all(sends)


def strips(s, e, n, d, m, ra, rb, u, so, eo, no):
    rows, cols = s.shape
    tiles = cols // LANES
    field = jax.ShapeDtypeStruct((rows, cols), F32)
    return pl.pallas_call(
        strip_kernel,
        out_shape=[field] * 3 + [jax.ShapeDtypeStruct((rows // SPACING, cols // SPACING), F32)],
        in_specs=[ANY] * 7 + [VMEM] + [ANY] * 3,
        out_specs=[ANY] * 3 + [VMEM],
        scratch_shapes=[pltpu.VMEM((tiles, 2 * STRIP + 2 * SUB, LANES), F32)] * 5
        + [
            pltpu.VMEM((tiles, 2 * STRIP + 2 * SUB, LANES), jnp.int32),
            pltpu.SemaphoreType.DMA((1,)),
            pltpu.SemaphoreType.DMA((1,)),
        ],
        input_output_aliases={8: 0, 9: 1, 10: 2},
        cost_estimate=pl.CostEstimate(flops=20 * rows * cols, bytes_accessed=16 * rows * cols, transcendentals=0),
        name="strips",
    )(s, e, n, d, m, ra, rb, u, so, eo, no)


def column_kernel(rc, rd, own, v, active, so_in, eo_in, no_in, so, eo, no, grad, S, E, N, Q, W, X, sem, osem):
    rows, cols = so.shape
    height = rows + 2 * HALO
    refs = (S, E, N, Q, W)
    even = is_even("lon")
    loads = []
    for f, src in enumerate((so_in, eo_in, no_in)):
        for end, col in enumerate((0, cols - LANES)):
            copy = pltpu.make_async_copy(src.at[:, col : col + LANES], X.at[f, end], sem.at[f, end])
            copy.start()
            loads.append(copy)
    zero_borders((S, N), height, 1)
    group = lax.div(lane_index(), HALO)

    def unpack(r):
        at = pl.ds(r - SUB, SUB)
        c, d = rc[at, :], rd[at, :]
        right, left = jnp.where(even, c, d), jnp.where(even, d, c)
        for f, dst in enumerate((S, E, N, Q)):
            a, b = right, left
            if f:
                a, b = pltpu.roll(a, LANES - f * HALO, 1), pltpu.roll(b, LANES - f * HALO, 1)
            tile = jnp.where(group == 2, a, jnp.where(group == 3, b, own[f, at, :]))
            dst[0, pl.ds(r, SUB), :] = tile
            if f == 3:
                W[0, pl.ds(r, SUB), :] = jnp.where(tile > 0.0, COURANT, 0.0)

    loop_rows(height // SUB, unpack, 20)
    for step in range(STEPS):
        loop_rows(height // SUB, lambda r: flux_rows(refs, r, 1), 20)
        loop_rows(height // SUB, lambda r: surface_rows(refs, r, 1, step == 0), 20)
    wait_all(loads)
    lane = lane_index()

    def merge(r):
        at = pl.ds(r - SUB, SUB)
        for f, src in enumerate((S, E, N)):
            tile = src[0, pl.ds(r + HALO, SUB), :]
            X[f, 0, at, :] = jnp.where(lane < EDGE, tile, X[f, 0, at, :])
            X[f, 1, at, :] = jnp.where(lane >= LANES - EDGE, pltpu.roll(tile, LANES // 2, 1), X[f, 1, at, :])

    loop_rows(rows // SUB, merge, 8)
    sends = []
    for f, dst in enumerate((so, eo, no)):
        for end, col in enumerate((0, cols - LANES)):
            copy = pltpu.make_async_copy(X.at[f, end], dst.at[:, col : col + LANES], osem.at[f, end])
            copy.start()
            sends.append(copy)
    points, across = grad.shape
    cell = lax.broadcasted_iota(jnp.int32, (points, height), 1) - HALO
    table = spline_of(cell, lax.broadcasted_iota(jnp.int32, (points, height), 0))
    part = dot(table, S[0, SUB : SUB + height, :])
    index = lax.broadcasted_iota(jnp.int32, (LANES, across), 0)
    col = jnp.where(index < HALO, index, jnp.where(index < 3 * HALO, index + (cols - 2 * HALO), index - LANES))
    weights = spline_of(col, lax.broadcasted_iota(jnp.int32, (LANES, across), 1))
    weights = jnp.where((col < EDGE) | (col >= cols - EDGE), weights, 0.0)
    sums = v[...] + dot(part, weights)
    grad[...] = sums * active[...].astype(F32) / SPACING
    wait_all(sends)


def columns(rc, rd, own, v, active, so, eo, no):
    rows, cols = so.shape
    height = rows + 2 * HALO
    field = jax.ShapeDtypeStruct((rows, cols), F32)
    return pl.pallas_call(
        column_kernel,
        out_shape=[field] * 3 + [jax.ShapeDtypeStruct(v.shape, F32)],
        in_specs=[VMEM] * 5 + [ANY] * 3,
        out_specs=[ANY] * 3 + [VMEM],
        scratch_shapes=[pltpu.VMEM((1, height + 2 * SUB, LANES), F32)] * 5
        + [
            pltpu.VMEM((3, 2, rows, LANES), F32),
            pltpu.SemaphoreType.DMA((3, 2)),
            pltpu.SemaphoreType.DMA((3, 2)),
        ],
        input_output_aliases={5: 0, 6: 1, 7: 2},
        name="columns",
    )(rc, rd, own, v, active, so, eo, no)


def swap(array, axis, offset):
    size = lax.axis_size(axis)
    pairs = []
    for i in range(offset, size):
        j = ((i - offset) ^ 1) + offset
        if j < size:
            pairs.append((i, j))
    return lax.ppermute(array, axis, pairs)


def local(surface_adjoint, east_adjoint, north_adjoint, water_depth, wet_mask, control_active):
    fields = (surface_adjoint, east_adjoint, north_adjoint, water_depth, wet_mask)
    pa, pb = pack_rows(*fields)
    rb = swap(pb, "lat", 1)
    ra = swap(pa, "lat", 0)
    so, eo, no, u, pc, pd, own = interior(*fields)
    pc, pd, own = corners(ra, rb, pc, pd, own)
    rc = swap(pc, "lon", 0)
    rd = swap(pd, "lon", 1)
    so, eo, no, v = strips(*fields, ra, rb, u, so, eo, no)
    return columns(rc, rd, own, v, control_active, so, eo, no)


def solution(mesh):
    spec = P("lat", "lon")
    return jax.shard_map(
        lambda *args: tuple(local(*args)),
        mesh=mesh,
        in_specs=(spec,) * 6,
        out_specs=(spec,) * 4,
        check_vma=False,
    )
```

```python
import functools

import jax
import jax.numpy as jnp
from jax import lax
from jax.experimental import pallas as pl
from jax.experimental.pallas import tpu as pltpu
from jax.sharding import PartitionSpec as P

SPACING = 16
STEPS = 3
COURANT = 0.5
LANES = 128
SUB = 8
HALO = 32
EDGE = 2 * STEPS
STRIP = HALO + 16
CHUNK = 64
F32 = jnp.float32
ANY = pl.BlockSpec(memory_space=pl.ANY)
HBM = pl.BlockSpec(memory_space=pltpu.HBM)
VMEM = pl.BlockSpec(memory_space=pltpu.VMEM)
PARAMS = pltpu.CompilerParams(vmem_limit_bytes=16 * 2**20)


def lane_index():
    return lax.broadcasted_iota(jnp.int32, (SUB, LANES), 1)


def east_minus_west(tiles):
    n = len(tiles)
    up = [pltpu.roll(t, LANES - 1, 1) for t in tiles]
    down = [pltpu.roll(t, 1, 1) for t in tiles]
    if n == 1:
        return [up[0] - down[0]]
    lane = lane_index()
    return [
        jnp.where(lane == LANES - 1, up[(c + 1) % n], up[c])
        - jnp.where(lane == 0, down[(c - 1) % n], down[c])
        for c in range(n)
    ]


def rows_at(ref, c, r):
    return ref[c, pl.ds(r, SUB), :]


def flux_rows(refs, r, tiles):
    S, E, N, Q, W = refs
    ds = east_minus_west([rows_at(S, c, r) for c in range(tiles)])
    for c in range(tiles):
        q = rows_at(Q, c, r)
        E[c, pl.ds(r, SUB), :] = rows_at(E, c, r) + q * ds[c]
        N[c, pl.ds(r, SUB), :] = rows_at(N, c, r) + q * (rows_at(S, c, r + 1) - rows_at(S, c, r - 1))


def surface_rows(refs, r, tiles, first):
    S, E, N, Q, W = refs
    de = east_minus_west([rows_at(E, c, r) for c in range(tiles)])
    for c in range(tiles):
        hw = rows_at(W, c, r)
        s = rows_at(S, c, r)
        if first:
            s = s * (hw + hw)
        S[c, pl.ds(r, SUB), :] = s + hw * (de[c] + (rows_at(N, c, r + 1) - rows_at(N, c, r - 1)))


def loop_rows(count, body, unroll=8):
    while count % unroll:
        unroll -= 1

    def step(i, carry):
        base = pl.multiple_of(i * (unroll * SUB), unroll * SUB) + SUB
        for u in range(unroll):
            body(base + u * SUB)
        return carry

    lax.fori_loop(0, count // unroll, step, 0)


def spline_weight(arg):
    mag = jnp.abs(arg)
    inner = 2.0 / 3.0 - mag * mag + 0.5 * mag * mag * mag
    outer = (2.0 - mag) * (2.0 - mag) * (2.0 - mag) / 6.0
    return jnp.where(mag < 1.0, inner, jnp.where(mag < 2.0, outer, 0.0 * mag))


def spline_of(cell, point):
    return spline_weight((cell.astype(F32) + 0.5) / SPACING - (point.astype(F32) + 0.5))


def dot(a, b):
    return jnp.dot(a, b, precision=lax.Precision.HIGHEST, preferred_element_type=F32)


def zero_borders(refs, rows, tiles):
    z = jnp.zeros((SUB, LANES), F32)
    for ref in refs:
        for c in range(tiles):
            ref[c, 0:SUB, :] = z
            ref[c, SUB + rows : SUB + rows + SUB, :] = z


def wait_all(copies):
    for copy in copies:
        copy.wait()


def is_even(axis):
    return lax.rem(lax.axis_index(axis), 2) == 0


def pack_rows_kernel(s, e, n, d, m, pa, pb, depth, mask, sem):
    rows = s.shape[0]
    even = is_even("lat")
    top = rows - HALO
    starts = (jnp.where(even, top, 0), jnp.where(even, 0, top))
    copies = []
    for side, (out, row) in enumerate(zip((pa, pb), starts)):
        at = pl.ds(pl.multiple_of(row, SUB), HALO)
        for f, (src, dst) in enumerate(
            (
                (s, out.at[0:HALO]),
                (e, out.at[HALO : 2 * HALO]),
                (n, out.at[2 * HALO : 3 * HALO]),
                (d, depth.at[side]),
                (m, mask.at[side]),
            )
        ):
            copy = pltpu.make_async_copy(src.at[at, :], dst, sem.at[side, f])
            copy.start()
            copies.append(copy)
    wait_all(copies)
    for side, out in enumerate((pa, pb)):
        wet = mask[side].astype(F32)
        out[HALO : 2 * HALO] = out[HALO : 2 * HALO] * wet
        out[2 * HALO : 3 * HALO] = out[2 * HALO : 3 * HALO] * wet
        out[3 * HALO : 4 * HALO] = depth[side] * (COURANT * wet)


def pack_rows(s, e, n, d, m):
    rows, cols = s.shape
    return pl.pallas_call(
        pack_rows_kernel,
        out_shape=[jax.ShapeDtypeStruct((4 * HALO, cols), F32)] * 2,
        in_specs=[HBM] * 5,
        out_specs=[VMEM] * 2,
        scratch_shapes=[
            pltpu.VMEM((2, HALO, cols), F32),
            pltpu.VMEM((2, HALO, cols), jnp.int32),
            pltpu.SemaphoreType.DMA((2, 5)),
        ],
        compiler_params=PARAMS,
        name="pack_rows",
    )(*(pltpu.with_memory_space_constraint(x, pltpu.HBM) for x in (s, e, n, d, m)))


def own_columns(first, last):
    lane = lane_index()
    both = jnp.where(lane < HALO, first, pltpu.roll(last, LANES // 2, 1))
    return jnp.where(lane < 2 * HALO, both, 0.0)


def pack_columns(own, even):
    group = lax.div(lane_index(), HALO)
    shift = jnp.where(even, 1, 0)
    pc = pd = None
    for f, tile in enumerate(own):
        turn = (f + 2) % 4
        moved = pltpu.roll(tile, turn * HALO, 1) if turn else tile
        if pc is None:
            pc = pd = moved
        else:
            pc = jnp.where(group == lax.rem(turn + shift, 4), moved, pc)
            pd = jnp.where(group == lax.rem(turn + 1 - shift, 4), moved, pd)
    return pc, pd


def interior_kernel(
    s, e, n, d, m, so, eo, no, u, pc, pd, own, S, E, N, Q, W, M, PC, PD, OWN, isem, osem, psem
):
    rows, cols = s.shape
    tiles = cols // LANES
    chunks = rows // CHUNK
    refs = (S, E, N, Q, W)
    even = is_even("lon")
    loads = []
    for k in range(chunks):
        copies = []
        for src, dst in ((s, S), (d, Q), (m, M), (e, E), (n, N)):
            for c in range(tiles):
                copy = pltpu.make_async_copy(
                    src.at[k * CHUNK : (k + 1) * CHUNK, c * LANES : (c + 1) * LANES],
                    dst.at[c, SUB + k * CHUNK : SUB + (k + 1) * CHUNK, :],
                    isem.at[k],
                )
                copy.start()
                copies.append(copy)
        loads.append(copies)
    zero_borders((S, N), rows, tiles)

    def first_flux(r):
        ds = east_minus_west([rows_at(S, c, r) for c in range(tiles)])
        ends = {}
        for c in range(tiles):
            wet = rows_at(M, c, r).astype(F32)
            hw = COURANT * wet
            q = rows_at(Q, c, r) * hw
            e0 = rows_at(E, c, r) * wet
            n0 = rows_at(N, c, r) * wet
            if c in (0, tiles - 1):
                ends[c] = (rows_at(S, c, r), e0, n0, q)
            W[c, pl.ds(r, SUB), :] = hw
            Q[c, pl.ds(r, SUB), :] = q
            E[c, pl.ds(r, SUB), :] = e0 + q * ds[c]
            N[c, pl.ds(r, SUB), :] = n0 + q * (rows_at(S, c, r + 1) - rows_at(S, c, r - 1))
        mine = [own_columns(a, b) for a, b in zip(ends[0], ends[tiles - 1])]
        for f in range(4):
            OWN[f, pl.ds(r - SUB, SUB), :] = mine[f]
        tc, td = pack_columns(mine, even)
        PC[pl.ds(r - SUB, SUB), :] = tc
        PD[pl.ds(r - SUB, SUB), :] = td

    def over_chunk(k, body):
        def shifted(r):
            body(r + k * CHUNK)

        loop_rows(CHUNK // SUB, shifted)

    wait_all(loads[0])
    for k in range(chunks):
        if k + 1 < chunks:
            wait_all(loads[k + 1])
        over_chunk(k, first_flux)
    sends = [
        pltpu.make_async_copy(PC, pc.at[HALO : HALO + rows], psem.at[0]),
        pltpu.make_async_copy(PD, pd.at[HALO : HALO + rows], psem.at[1]),
        pltpu.make_async_copy(OWN, own.at[:, HALO : HALO + rows], psem.at[2]),
    ]
    for copy in sends:
        copy.start()
    loop_rows(rows // SUB, lambda r: surface_rows(refs, r, tiles, True))
    for step in range(1, STEPS):
        last = step == STEPS - 1
        for k in range(chunks):
            over_chunk(k, lambda r: flux_rows(refs, r, tiles))
            if last:
                sends += store_rows(((E, eo), (N, no)), k, tiles, osem)
        for k in range(chunks):
            over_chunk(k, lambda r: surface_rows(refs, r, tiles, False))
            if last:
                sends += store_rows(((S, so),), k, tiles, osem)
    points = rows // SPACING
    cell = lax.broadcasted_iota(jnp.int32, (points, rows), 1)
    table = spline_of(cell, lax.broadcasted_iota(jnp.int32, (points, rows), 0))
    table = jnp.where((cell >= EDGE) & (cell < rows - EDGE), table, 0.0)
    for c in range(tiles):
        u[:, c * LANES : (c + 1) * LANES] = dot(table, S[c, SUB : SUB + rows, :])
    wait_all(sends)


def store_rows(pairs, k, tiles, sem):
    copies = []
    for src, dst in pairs:
        for c in range(tiles):
            copy = pltpu.make_async_copy(
                src.at[c, SUB + k * CHUNK : SUB + (k + 1) * CHUNK, :],
                dst.at[k * CHUNK : (k + 1) * CHUNK, c * LANES : (c + 1) * LANES],
                sem.at[0],
            )
            copy.start()
            copies.append(copy)
    return copies


def interior(s, e, n, d, m):
    rows, cols = s.shape
    tiles = cols // LANES
    field = jax.ShapeDtypeStruct((rows, cols), F32)
    wide = jax.ShapeDtypeStruct((rows + 2 * HALO, LANES), F32)
    return pl.pallas_call(
        interior_kernel,
        out_shape=[field] * 3
        + [
            jax.ShapeDtypeStruct((rows // SPACING, cols), F32),
            wide,
            wide,
            jax.ShapeDtypeStruct((4, rows + 2 * HALO, LANES), F32),
        ],
        in_specs=[ANY] * 5,
        out_specs=[ANY] * 3 + [VMEM] + [ANY] * 3,
        scratch_shapes=[pltpu.VMEM((tiles, rows + 2 * SUB, LANES), F32)] * 5
        + [
            pltpu.VMEM((tiles, rows + 2 * SUB, LANES), jnp.int32),
            pltpu.VMEM((rows, LANES), F32),
            pltpu.VMEM((rows, LANES), F32),
            pltpu.VMEM((4, rows, LANES), F32),
            pltpu.SemaphoreType.DMA((rows // CHUNK,)),
            pltpu.SemaphoreType.DMA((1,)),
            pltpu.SemaphoreType.DMA((3,)),
        ],
        cost_estimate=pl.CostEstimate(flops=40 * rows * cols, bytes_accessed=32 * rows * cols, transcendentals=0),
        compiler_params=PARAMS,
        name="interior",
    )(s, e, n, d, m)


def corner_kernel(ra, rb, pc_in, pd_in, own_in, pc, pd, own, X, PC, PD, OWN, sem, psem):
    del pc_in, pd_in, own_in
    height = pc.shape[0]
    cols = ra.shape[1]
    even, lon_even = is_even("lat"), is_even("lon")
    copies = []
    for side, src in enumerate((ra, rb)):
        for end, col in enumerate((0, cols - LANES)):
            copy = pltpu.make_async_copy(src.at[:, col : col + LANES], X.at[side, end], sem.at[side, end])
            copy.start()
            copies.append(copy)
    wait_all(copies)
    top = height - HALO
    starts = (jnp.where(even, top, 0), jnp.where(even, 0, top))
    sends = []
    for side, row in enumerate(starts):
        for r in range(0, HALO, SUB):
            mine = [
                own_columns(X[side, 0, f * HALO + r : f * HALO + r + SUB, :], X[side, 1, f * HALO + r : f * HALO + r + SUB, :])
                for f in range(4)
            ]
            for f in range(4):
                OWN[side, f, r : r + SUB, :] = mine[f]
            tc, td = pack_columns(mine, lon_even)
            PC[side, r : r + SUB, :] = tc
            PD[side, r : r + SUB, :] = td
        at = pl.ds(pl.multiple_of(row, SUB), HALO)
        for f, (src, dst) in enumerate(
            ((PC.at[side], pc.at[at, :]), (PD.at[side], pd.at[at, :]), (OWN.at[side], own.at[:, at, :]))
        ):
            copy = pltpu.make_async_copy(src, dst, psem.at[side, f])
            copy.start()
            sends.append(copy)
    wait_all(sends)


def corners(ra, rb, pc, pd, own):
    return pl.pallas_call(
        corner_kernel,
        out_shape=[jax.ShapeDtypeStruct(x.shape, F32) for x in (pc, pd, own)],
        in_specs=[ANY] * 5,
        out_specs=[ANY] * 3,
        scratch_shapes=[
            pltpu.VMEM((2, 2, 4 * HALO, LANES), F32),
            pltpu.VMEM((2, HALO, LANES), F32),
            pltpu.VMEM((2, HALO, LANES), F32),
            pltpu.VMEM((2, 4, HALO, LANES), F32),
            pltpu.SemaphoreType.DMA((2, 2)),
            pltpu.SemaphoreType.DMA((2, 3)),
        ],
        input_output_aliases={2: 0, 3: 1, 4: 2},
        compiler_params=PARAMS,
        name="corners",
    )(ra, rb, pc, pd, own)


def strip_kernel(s, e, n, d, m, ra, rb, u, so_in, eo_in, no_in, so, eo, no, v, S, E, N, Q, W, M, sem, osem):
    del so_in, eo_in, no_in
    rows, cols = s.shape
    tiles = cols // LANES
    refs = (S, E, N, Q, W)
    even = is_even("lat")
    keep = STRIP - HALO
    count = 2 * STRIP
    loads = []
    for src, dst in ((s, S), (e, E), (n, N), (d, Q), (m, M)):
        for row, to in ((0, HALO), (rows - keep, STRIP)):
            for c in range(tiles):
                copy = pltpu.make_async_copy(
                    src.at[row : row + keep, c * LANES : (c + 1) * LANES],
                    dst.at[c, SUB + to : SUB + to + keep, :],
                    sem.at[0],
                )
                copy.start()
                loads.append(copy)
    high = SUB + STRIP + keep
    for src, to in ((ra, jnp.where(even, high, SUB)), (rb, jnp.where(even, SUB, high))):
        at = pl.ds(pl.multiple_of(to, SUB), HALO)
        for f, dst in enumerate((S, E, N, Q)):
            for c in range(tiles):
                copy = pltpu.make_async_copy(
                    src.at[f * HALO : (f + 1) * HALO, c * LANES : (c + 1) * LANES],
                    dst.at[c, at, :],
                    sem.at[0],
                )
                copy.start()
                loads.append(copy)
    zero_borders((S, N), count, tiles)
    wait_all(loads)
    for c in range(tiles):
        for r in range(SUB + HALO, SUB + HALO + 2 * keep, SUB):
            wet = M[c, r : r + SUB, :].astype(F32)
            hw = COURANT * wet
            W[c, r : r + SUB, :] = hw
            Q[c, r : r + SUB, :] = Q[c, r : r + SUB, :] * hw
            E[c, r : r + SUB, :] = E[c, r : r + SUB, :] * wet
            N[c, r : r + SUB, :] = N[c, r : r + SUB, :] * wet
        for first in (SUB, high):
            for r in range(first, first + HALO, SUB):
                W[c, r : r + SUB, :] = jnp.where(Q[c, r : r + SUB, :] > 0.0, COURANT, 0.0)
    for step in range(STEPS):
        loop_rows(count // SUB, lambda r: flux_rows(refs, r, tiles), 12)
        loop_rows(count // SUB, lambda r: surface_rows(refs, r, tiles, step == 0), 12)
    sends = []
    for src, dst in ((S, so), (E, eo), (N, no)):
        for frm, to in ((SUB + HALO, 0), (SUB + STRIP + keep - SUB, rows - SUB)):
            for c in range(tiles):
                copy = pltpu.make_async_copy(
                    src.at[c, frm : frm + SUB, :],
                    dst.at[to : to + SUB, c * LANES : (c + 1) * LANES],
                    osem.at[0],
                )
                copy.start()
                sends.append(copy)
    points = rows // SPACING
    index = lax.broadcasted_iota(jnp.int32, (points, count), 1)
    cell = jnp.where(index < STRIP, index - HALO, index + (rows - keep - STRIP))
    table = spline_of(cell, lax.broadcasted_iota(jnp.int32, (points, count), 0))
    table = jnp.where((cell < EDGE) | (cell >= rows - EDGE), table, 0.0)
    across = cols // SPACING
    total = jnp.zeros((points, across), F32)
    for c in range(tiles):
        part = u[:, c * LANES : (c + 1) * LANES] + dot(table, S[c, SUB : SUB + count, :])
        col = lax.broadcasted_iota(jnp.int32, (LANES, across), 0) + c * LANES
        weights = spline_of(col, lax.broadcasted_iota(jnp.int32, (LANES, across), 1))
        weights = jnp.where((col >= EDGE) & (col < cols - EDGE), weights, 0.0)
        total = total + dot(part, weights)
    v[...] = total
    wait_all(sends)


def strips(s, e, n, d, m, ra, rb, u, so, eo, no):
    rows, cols = s.shape
    tiles = cols // LANES
    field = jax.ShapeDtypeStruct((rows, cols), F32)
    return pl.pallas_call(
        strip_kernel,
        out_shape=[field] * 3 + [jax.ShapeDtypeStruct((rows // SPACING, cols // SPACING), F32)],
        in_specs=[ANY] * 7 + [VMEM] + [ANY] * 3,
        out_specs=[ANY] * 3 + [VMEM],
        scratch_shapes=[pltpu.VMEM((tiles, 2 * STRIP + 2 * SUB, LANES), F32)] * 5
        + [
            pltpu.VMEM((tiles, 2 * STRIP + 2 * SUB, LANES), jnp.int32),
            pltpu.SemaphoreType.DMA((1,)),
            pltpu.SemaphoreType.DMA((1,)),
        ],
        input_output_aliases={8: 0, 9: 1, 10: 2},
        cost_estimate=pl.CostEstimate(flops=20 * rows * cols, bytes_accessed=16 * rows * cols, transcendentals=0),
        compiler_params=PARAMS,
        name="strips",
    )(s, e, n, d, m, ra, rb, u, so, eo, no)


def column_kernel(rc, rd, own, v, active, so_in, eo_in, no_in, so, eo, no, grad, S, E, N, Q, W, X, sem, osem):
    rows, cols = so.shape
    height = rows + 2 * HALO
    refs = (S, E, N, Q, W)
    even = is_even("lon")
    loads = []
    for f, src in enumerate((so_in, eo_in, no_in)):
        for end, col in enumerate((0, cols - LANES)):
            copy = pltpu.make_async_copy(src.at[:, col : col + LANES], X.at[f, end], sem.at[f, end])
            copy.start()
            loads.append(copy)
    zero_borders((S, N), height, 1)
    group = lax.div(lane_index(), HALO)

    def unpack(r):
        at = pl.ds(r - SUB, SUB)
        c, d = rc[at, :], rd[at, :]
        right, left = jnp.where(even, c, d), jnp.where(even, d, c)
        for f, dst in enumerate((S, E, N, Q)):
            a, b = right, left
            if f:
                a, b = pltpu.roll(a, LANES - f * HALO, 1), pltpu.roll(b, LANES - f * HALO, 1)
            tile = jnp.where(group == 2, a, jnp.where(group == 3, b, own[f, at, :]))
            dst[0, pl.ds(r, SUB), :] = tile
            if f == 3:
                W[0, pl.ds(r, SUB), :] = jnp.where(tile > 0.0, COURANT, 0.0)

    loop_rows(height // SUB, unpack, 20)
    for step in range(STEPS):
        loop_rows(height // SUB, lambda r: flux_rows(refs, r, 1), 20)
        loop_rows(height // SUB, lambda r: surface_rows(refs, r, 1, step == 0), 20)
    wait_all(loads)
    lane = lane_index()

    def merge(r):
        at = pl.ds(r - SUB, SUB)
        for f, src in enumerate((S, E, N)):
            tile = src[0, pl.ds(r + HALO, SUB), :]
            X[f, 0, at, :] = jnp.where(lane < EDGE, tile, X[f, 0, at, :])
            X[f, 1, at, :] = jnp.where(lane >= LANES - EDGE, pltpu.roll(tile, LANES // 2, 1), X[f, 1, at, :])

    loop_rows(rows // SUB, merge, 8)
    sends = []
    for f, dst in enumerate((so, eo, no)):
        for end, col in enumerate((0, cols - LANES)):
            copy = pltpu.make_async_copy(X.at[f, end], dst.at[:, col : col + LANES], osem.at[f, end])
            copy.start()
            sends.append(copy)
    points, across = grad.shape
    cell = lax.broadcasted_iota(jnp.int32, (points, height), 1) - HALO
    table = spline_of(cell, lax.broadcasted_iota(jnp.int32, (points, height), 0))
    part = dot(table, S[0, SUB : SUB + height, :])
    index = lax.broadcasted_iota(jnp.int32, (LANES, across), 0)
    col = jnp.where(index < HALO, index, jnp.where(index < 3 * HALO, index + (cols - 2 * HALO), index - LANES))
    weights = spline_of(col, lax.broadcasted_iota(jnp.int32, (LANES, across), 1))
    weights = jnp.where((col < EDGE) | (col >= cols - EDGE), weights, 0.0)
    sums = v[...] + dot(part, weights)
    grad[...] = sums * active[...].astype(F32) / SPACING
    wait_all(sends)


def columns(rc, rd, own, v, active, so, eo, no):
    rows, cols = so.shape
    height = rows + 2 * HALO
    field = jax.ShapeDtypeStruct((rows, cols), F32)
    return pl.pallas_call(
        column_kernel,
        out_shape=[field] * 3 + [jax.ShapeDtypeStruct(v.shape, F32)],
        in_specs=[VMEM] * 5 + [ANY] * 3,
        out_specs=[ANY] * 3 + [VMEM],
        scratch_shapes=[pltpu.VMEM((1, height + 2 * SUB, LANES), F32)] * 5
        + [
            pltpu.VMEM((3, 2, rows, LANES), F32),
            pltpu.SemaphoreType.DMA((3, 2)),
            pltpu.SemaphoreType.DMA((3, 2)),
        ],
        input_output_aliases={5: 0, 6: 1, 7: 2},
        compiler_params=PARAMS,
        name="columns",
    )(rc, rd, own, v, active, so, eo, no)


def swap(array, axis, offset):
    size = lax.axis_size(axis)
    pairs = []
    for i in range(offset, size):
        j = ((i - offset) ^ 1) + offset
        if j < size:
            pairs.append((i, j))
    return lax.ppermute(array, axis, pairs)


def local(surface_adjoint, east_adjoint, north_adjoint, water_depth, wet_mask, control_active):
    fields = (surface_adjoint, east_adjoint, north_adjoint, water_depth, wet_mask)
    pa, pb = pack_rows(*fields)
    rb = swap(pb, "lat", 1)
    ra = swap(pa, "lat", 0)
    so, eo, no, u, pc, pd, own = interior(*fields)
    pc, pd, own = corners(ra, rb, pc, pd, own)
    rc = swap(pc, "lon", 0)
    rd = swap(pd, "lon", 1)
    so, eo, no, v = strips(*fields, ra, rb, u, so, eo, no)
    return columns(rc, rd, own, v, control_active, so, eo, no)


def solution(mesh):
    spec = P("lat", "lon")
    return jax.shard_map(
        lambda *args: tuple(local(*args)),
        mesh=mesh,
        in_specs=(spec,) * 6,
        out_specs=(spec,) * 4,
        check_vma=False,
    )
```

```python
import functools

import jax
import jax.numpy as jnp
from jax import lax
from jax.experimental import pallas as pl
from jax.experimental.pallas import tpu as pltpu
from jax.sharding import PartitionSpec as P

SPACING = 16
STEPS = 3
COURANT = 0.5
LANES = 128
SUB = 8
HALO = 32
EDGE = 2 * STEPS
STRIP = HALO + 16
CHUNK = 64
F32 = jnp.float32
ANY = pl.BlockSpec(memory_space=pl.ANY)
HBM = pl.BlockSpec(memory_space=pltpu.HBM)
VMEM = pl.BlockSpec(memory_space=pltpu.VMEM)
PARAMS = pltpu.CompilerParams(vmem_limit_bytes=16 * 2**20)


def lane_index():
    return lax.broadcasted_iota(jnp.int32, (SUB, LANES), 1)


def east_minus_west(tiles):
    n = len(tiles)
    up = [pltpu.roll(t, LANES - 1, 1) for t in tiles]
    down = [pltpu.roll(t, 1, 1) for t in tiles]
    if n == 1:
        return [up[0] - down[0]]
    lane = lane_index()
    return [
        jnp.where(lane == LANES - 1, up[(c + 1) % n], up[c])
        - jnp.where(lane == 0, down[(c - 1) % n], down[c])
        for c in range(n)
    ]


def rows_at(ref, c, r):
    return ref[c, pl.ds(r, SUB), :]


def flux_rows(refs, r, tiles):
    S, E, N, Q, W = refs
    ds = east_minus_west([rows_at(S, c, r) for c in range(tiles)])
    for c in range(tiles):
        q = rows_at(Q, c, r)
        E[c, pl.ds(r, SUB), :] = rows_at(E, c, r) + q * ds[c]
        N[c, pl.ds(r, SUB), :] = rows_at(N, c, r) + q * (rows_at(S, c, r + 1) - rows_at(S, c, r - 1))


def surface_rows(refs, r, tiles, first):
    S, E, N, Q, W = refs
    de = east_minus_west([rows_at(E, c, r) for c in range(tiles)])
    for c in range(tiles):
        hw = rows_at(W, c, r)
        s = rows_at(S, c, r)
        if first:
            s = s * (hw + hw)
        S[c, pl.ds(r, SUB), :] = s + hw * (de[c] + (rows_at(N, c, r + 1) - rows_at(N, c, r - 1)))


def loop_rows(count, body, unroll=64):
    if unroll >= count:
        for i in range(count):
            body(SUB + i * SUB)
        return
    while count % unroll:
        unroll -= 1

    def step(i, carry):
        base = pl.multiple_of(i * (unroll * SUB), unroll * SUB) + SUB
        for u in range(unroll):
            body(base + u * SUB)
        return carry

    lax.fori_loop(0, count // unroll, step, 0)


def spline_weight(arg):
    mag = jnp.abs(arg)
    inner = 2.0 / 3.0 - mag * mag + 0.5 * mag * mag * mag
    outer = (2.0 - mag) * (2.0 - mag) * (2.0 - mag) / 6.0
    return jnp.where(mag < 1.0, inner, jnp.where(mag < 2.0, outer, 0.0 * mag))


def spline_of(cell, point):
    return spline_weight((cell.astype(F32) + 0.5) / SPACING - (point.astype(F32) + 0.5))


def dot(a, b):
    return jnp.dot(a, b, precision=lax.Precision.HIGHEST, preferred_element_type=F32)


def zero_borders(refs, rows, tiles):
    z = jnp.zeros((SUB, LANES), F32)
    for ref in refs:
        for c in range(tiles):
            ref[c, 0:SUB, :] = z
            ref[c, SUB + rows : SUB + rows + SUB, :] = z


def wait_all(copies):
    for copy in copies:
        copy.wait()


def is_even(axis):
    return lax.rem(lax.axis_index(axis), 2) == 0


def own_columns(first, last):
    lane = lane_index()
    both = jnp.where(lane < HALO, first, pltpu.roll(last, LANES // 2, 1))
    return jnp.where(lane < 2 * HALO, both, 0.0)


def masked(s, e, n, d, wet):
    return s, e * wet, n * wet, d * (COURANT * wet)


def pack_first_kernel(s, e, n, d, m, pa, pc, depth, mask, C, M, sem):
    rows, cols = s.shape
    even = is_even("lat")
    top = rows - HALO
    near, far = jnp.where(even, top, 0), jnp.where(even, 0, top)
    far = pl.ds(pl.multiple_of(far, SUB), HALO)
    near = pl.ds(pl.multiple_of(near, SUB), HALO)
    copies = []
    for f, src in enumerate((s, e, n, d, m)):
        for end, col in enumerate((0, cols - LANES)):
            dst = M.at[end] if f == 4 else C.at[f, end]
            copies.append(pltpu.make_async_copy(src.at[far, col : col + LANES], dst, sem.at[0]))
    for src, dst in (
        (s, pa.at[0:HALO]),
        (e, pa.at[HALO : 2 * HALO]),
        (n, pa.at[2 * HALO : 3 * HALO]),
        (d, depth),
        (m, mask),
    ):
        copies.append(pltpu.make_async_copy(src.at[near, :], dst, sem.at[1]))
    for copy in copies:
        copy.start()
    wait_all(copies[:10])
    for r in range(0, HALO, SUB):
        ends = [
            masked(*(C[f, end, r : r + SUB, :] for f in range(4)), M[end, r : r + SUB, :].astype(F32))
            for end in range(2)
        ]
        mine = [own_columns(a, b) for a, b in zip(*ends)]
        for half in range(2):
            pair = mine[2 * half] + pltpu.roll(mine[2 * half + 1], LANES // 2, 1)
            pc[half * HALO + r : half * HALO + r + SUB, :] = pair
    wait_all(copies[10:])
    wet = mask[...].astype(F32)
    pa[HALO : 2 * HALO] = pa[HALO : 2 * HALO] * wet
    pa[2 * HALO : 3 * HALO] = pa[2 * HALO : 3 * HALO] * wet
    pa[3 * HALO : 4 * HALO] = depth[...] * (COURANT * wet)


def pack_first(s, e, n, d, m):
    rows, cols = s.shape
    return pl.pallas_call(
        pack_first_kernel,
        out_shape=[jax.ShapeDtypeStruct((4 * HALO, cols), F32), jax.ShapeDtypeStruct((2 * HALO, LANES), F32)],
        in_specs=[ANY] * 5,
        out_specs=[VMEM] * 2,
        scratch_shapes=[
            pltpu.VMEM((HALO, cols), F32),
            pltpu.VMEM((HALO, cols), jnp.int32),
            pltpu.VMEM((4, 2, HALO, LANES), F32),
            pltpu.VMEM((2, HALO, LANES), jnp.int32),
            pltpu.SemaphoreType.DMA((2,)),
        ],
        compiler_params=PARAMS,
        name="pack_first",
    )(*(in_hbm(x) for x in (s, e, n, d, m)))


def in_hbm(x):
    return pltpu.with_memory_space_constraint(x, pltpu.HBM)


def pack_columns(own, even):
    group = lax.div(lane_index(), HALO)
    shift = jnp.where(even, 1, 0)
    pc = pd = None
    for f, tile in enumerate(own):
        turn = (f + 2) % 4
        moved = pltpu.roll(tile, turn * HALO, 1) if turn else tile
        if pc is None:
            pc = pd = moved
        else:
            pc = jnp.where(group == lax.rem(turn + shift, 4), moved, pc)
            pd = jnp.where(group == lax.rem(turn + 1 - shift, 4), moved, pd)
    return pc, pd


def edge_kernel(s, e, n, d, m, pb, pc, pd, own, PC, PD, OWN, sem):
    rows, cols = s.shape
    lat_even, lon_even = is_even("lat"), is_even("lon")
    far = pl.multiple_of(jnp.where(lat_even, 0, rows - HALO), SUB)
    for r in range(0, HALO, SUB):
        at = pl.ds(far + r, SUB)
        wet = m[at, :].astype(F32)
        for f, value in enumerate(masked(s[at, :], e[at, :], n[at, :], d[at, :], wet)):
            pb[f * HALO + r : f * HALO + r + SUB, :] = value

    def pack(r):
        at = pl.ds(r - SUB, SUB)
        ends = []
        for col in (0, cols - LANES):
            to = slice(col, col + LANES)
            ends.append(masked(s[at, to], e[at, to], n[at, to], d[at, to], m[at, to].astype(F32)))
        mine = [own_columns(a, b) for a, b in zip(*ends)]
        for f in range(4):
            OWN[f, at, :] = mine[f]
        PC[at, :], PD[at, :] = pack_columns(mine, lon_even)

    loop_rows(rows // SUB, pack, 8)
    sends = [
        pltpu.make_async_copy(PC, pc.at[HALO : HALO + rows], sem.at[0]),
        pltpu.make_async_copy(PD, pd.at[HALO : HALO + rows], sem.at[1]),
        pltpu.make_async_copy(OWN, own.at[:, HALO : HALO + rows], sem.at[2]),
    ]
    for copy in sends:
        copy.start()
    wait_all(sends)


def edges(s, e, n, d, m):
    rows, cols = s.shape
    wide = jax.ShapeDtypeStruct((rows + 2 * HALO, LANES), F32)
    return pl.pallas_call(
        edge_kernel,
        out_shape=[
            jax.ShapeDtypeStruct((4 * HALO, cols), F32),
            wide,
            wide,
            jax.ShapeDtypeStruct((4, rows + 2 * HALO, LANES), F32),
        ],
        in_specs=[VMEM] * 5,
        out_specs=[VMEM] + [ANY] * 3,
        scratch_shapes=[
            pltpu.VMEM((rows, LANES), F32),
            pltpu.VMEM((rows, LANES), F32),
            pltpu.VMEM((4, rows, LANES), F32),
            pltpu.SemaphoreType.DMA((3,)),
        ],
        compiler_params=PARAMS,
        name="edges",
    )(s, e, n, d, m)


def corner_kernel(ra, rbc, pc_in, pd_in, own_in, pc, pd, own, PC, PD, OWN, sem):
    del pc_in, pd_in, own_in
    height = pc.shape[0]
    cols = ra.shape[1]
    even, lon_even = is_even("lat"), is_even("lon")
    top = height - HALO
    starts = (jnp.where(even, top, 0), jnp.where(even, 0, top))
    sends = []
    lane = lane_index()
    for side, row in enumerate(starts):
        for r in range(0, HALO, SUB):
            if side == 0:
                mine = [
                    own_columns(
                        ra[f * HALO + r : f * HALO + r + SUB, 0:LANES],
                        ra[f * HALO + r : f * HALO + r + SUB, cols - LANES : cols],
                    )
                    for f in range(4)
                ]
            else:
                mine = []
                for half in range(2):
                    pair = rbc[half * HALO + r : half * HALO + r + SUB, :]
                    for tile in (pair, pltpu.roll(pair, LANES // 2, 1)):
                        mine.append(jnp.where(lane < 2 * HALO, tile, 0.0))
            for f in range(4):
                OWN[side, f, r : r + SUB, :] = mine[f]
            PC[side, r : r + SUB, :], PD[side, r : r + SUB, :] = pack_columns(mine, lon_even)
        at = pl.ds(pl.multiple_of(row, SUB), HALO)
        for f, (src, dst) in enumerate(
            ((PC.at[side], pc.at[at, :]), (PD.at[side], pd.at[at, :]), (OWN.at[side], own.at[:, at, :]))
        ):
            copy = pltpu.make_async_copy(src, dst, sem.at[side, f])
            copy.start()
            sends.append(copy)
    wait_all(sends)


def corners(ra, rbc, pc, pd, own):
    return pl.pallas_call(
        corner_kernel,
        out_shape=[jax.ShapeDtypeStruct(x.shape, F32) for x in (pc, pd, own)],
        in_specs=[VMEM] * 2 + [ANY] * 3,
        out_specs=[ANY] * 3,
        scratch_shapes=[
            pltpu.VMEM((2, HALO, LANES), F32),
            pltpu.VMEM((2, HALO, LANES), F32),
            pltpu.VMEM((2, 4, HALO, LANES), F32),
            pltpu.SemaphoreType.DMA((2, 3)),
        ],
        input_output_aliases={2: 0, 3: 1, 4: 2},
        compiler_params=PARAMS,
        name="corners",
    )(ra, rbc, pc, pd, own)


def interior_kernel(s, e, n, d, m, S, E, N, u, Q, W, isem):
    rows, cols = e.shape
    tiles = cols // LANES
    chunks = rows // CHUNK
    refs = (S, E, N, Q, W)
    loads = []
    for k in range(chunks):
        loads.append([])
        for c in range(tiles):
            copy = pltpu.make_async_copy(
                s.at[k * CHUNK : (k + 1) * CHUNK, c * LANES : (c + 1) * LANES],
                S.at[c, SUB + k * CHUNK : SUB + (k + 1) * CHUNK, :],
                isem.at[k],
            )
            copy.start()
            loads[-1].append(copy)
    zero_borders((S, N), rows, tiles)

    def first_flux(r):
        ds = east_minus_west([rows_at(S, c, r) for c in range(tiles)])
        at = pl.ds(r - SUB, SUB)
        for c in range(tiles):
            to = slice(c * LANES, (c + 1) * LANES)
            wet = m[at, to].astype(F32)
            hw = COURANT * wet
            q = d[at, to] * hw
            W[c, pl.ds(r, SUB), :] = hw
            Q[c, pl.ds(r, SUB), :] = q
            E[c, pl.ds(r, SUB), :] = e[at, to] * wet + q * ds[c]
            N[c, pl.ds(r, SUB), :] = n[at, to] * wet + q * (rows_at(S, c, r + 1) - rows_at(S, c, r - 1))

    def over_chunk(k, body):
        def shifted(r):
            body(pl.multiple_of(r + k * CHUNK, SUB))

        loop_rows(CHUNK // SUB, shifted)

    wait_all(loads[0])
    for k in range(chunks):
        if k + 1 < chunks:
            wait_all(loads[k + 1])
        over_chunk(k, first_flux)
    loop_rows(rows // SUB, lambda r: surface_rows(refs, r, tiles, True))
    for step in range(1, STEPS):
        loop_rows(rows // SUB, lambda r: flux_rows(refs, r, tiles))
        loop_rows(rows // SUB, lambda r: surface_rows(refs, r, tiles, False))
    points = rows // SPACING
    cell = lax.broadcasted_iota(jnp.int32, (points, rows), 1)
    table = spline_of(cell, lax.broadcasted_iota(jnp.int32, (points, rows), 0))
    table = jnp.where((cell >= EDGE) & (cell < rows - EDGE), table, 0.0)
    for c in range(tiles):
        u[:, c * LANES : (c + 1) * LANES] = dot(table, S[c, SUB : SUB + rows, :])


def interior(s, e, n, d, m):
    rows, cols = s.shape
    tiles = cols // LANES
    field = (tiles, rows + 2 * SUB, LANES)
    return pl.pallas_call(
        interior_kernel,
        out_shape=[jax.ShapeDtypeStruct(field, F32)] * 3 + [jax.ShapeDtypeStruct((rows // SPACING, cols), F32)],
        in_specs=[ANY] + [VMEM] * 4,
        out_specs=[VMEM] * 4,
        scratch_shapes=[pltpu.VMEM(field, F32)] * 2 + [pltpu.SemaphoreType.DMA((rows // CHUNK,))],
        cost_estimate=pl.CostEstimate(flops=40 * rows * cols, bytes_accessed=32 * rows * cols, transcendentals=0),
        compiler_params=PARAMS,
        name="interior",
    )(s, e, n, d, m)


def strip_kernel(s, e, n, d, m, ra, rb, u, si, ei, ni, so, eo, no, v, x, S, E, N, Q, W, osem):
    rows, cols = s.shape
    tiles = cols // LANES
    refs = (S, E, N, Q, W)
    even = is_even("lat")
    keep = STRIP - HALO
    count = 2 * STRIP
    sends = []
    for src, dst in ((ei, eo), (ni, no), (si, so)):
        for c in range(1, tiles - 1):
            copy = pltpu.make_async_copy(
                src.at[c, 2 * SUB : rows, :], dst.at[SUB : rows - SUB, c * LANES : (c + 1) * LANES], osem.at[0]
            )
            copy.start()
            sends.append(copy)
    zero_borders((S, N), count, tiles)
    for row, to in ((0, SUB + HALO), (rows - keep, SUB + STRIP)):
        for r in range(0, keep, SUB):
            for c in range(tiles):
                at, lanes = slice(row + r, row + r + SUB), slice(c * LANES, (c + 1) * LANES)
                wet = m[at, lanes].astype(F32)
                hw = COURANT * wet
                here = slice(to + r, to + r + SUB)
                S[c, here, :] = s[at, lanes]
                E[c, here, :] = e[at, lanes] * wet
                N[c, here, :] = n[at, lanes] * wet
                Q[c, here, :] = d[at, lanes] * hw
                W[c, here, :] = hw
    high = SUB + STRIP + keep
    for src, to in ((ra, jnp.where(even, high, SUB)), (rb, jnp.where(even, SUB, high))):
        for r in range(0, HALO, SUB):
            here = pl.ds(pl.multiple_of(to + r, SUB), SUB)
            for c in range(tiles):
                for f, dst in enumerate((S, E, N, Q)):
                    value = src[f * HALO + r : f * HALO + r + SUB, c * LANES : (c + 1) * LANES]
                    dst[c, here, :] = value
                W[c, here, :] = jnp.where(value > 0.0, COURANT, 0.0)
    for step in range(STEPS):
        loop_rows(count // SUB, lambda r: flux_rows(refs, r, tiles), 12)
        loop_rows(count // SUB, lambda r: surface_rows(refs, r, tiles, step == 0), 12)
    for f, (src, dst) in enumerate(((S, so), (E, eo), (N, no))):
        for side, (frm, to) in enumerate(((SUB + HALO, 0), (SUB + STRIP + keep - SUB, rows - SUB))):
            for c in range(tiles):
                if c in (0, tiles - 1):
                    x[f, min(c, 1), side] = src[c, frm : frm + SUB, :]
                    continue
                copy = pltpu.make_async_copy(
                    src.at[c, frm : frm + SUB, :],
                    dst.at[to : to + SUB, c * LANES : (c + 1) * LANES],
                    osem.at[0],
                )
                copy.start()
                sends.append(copy)
    points = rows // SPACING
    index = lax.broadcasted_iota(jnp.int32, (points, count), 1)
    cell = jnp.where(index < STRIP, index - HALO, index + (rows - keep - STRIP))
    table = spline_of(cell, lax.broadcasted_iota(jnp.int32, (points, count), 0))
    table = jnp.where((cell < EDGE) | (cell >= rows - EDGE), table, 0.0)
    lane = lax.broadcasted_iota(jnp.int32, (points, LANES), 1)
    parts = []
    for c in range(tiles):
        part = u[:, c * LANES : (c + 1) * LANES] + dot(table, S[c, SUB : SUB + count, :])
        if c == 0:
            part = jnp.where(lane < EDGE, 0.0, part)
        if c == tiles - 1:
            part = jnp.where(lane >= LANES - EDGE, 0.0, part)
        parts.append(part)
    weights = spline_of(
        lax.broadcasted_iota(jnp.int32, (LANES, LANES), 0),
        lax.broadcasted_iota(jnp.int32, (LANES, LANES), 1) - 2,
    )
    product = dot(jnp.concatenate(parts, axis=0), weights)
    total = jnp.zeros((points, LANES), F32)
    reach = LANES // SPACING + 4
    for c in range(tiles):
        piece = jnp.where(lane < reach, product[c * points : (c + 1) * points], 0.0)
        total = total + pltpu.roll(piece, (c * (LANES // SPACING) - 2) % LANES, 1)
    v[...] = total
    wait_all(sends)


def strips(s, e, n, d, m, ra, rb, u, si, ei, ni):
    rows, cols = s.shape
    tiles = cols // LANES
    field = jax.ShapeDtypeStruct((rows, cols), F32)
    return pl.pallas_call(
        strip_kernel,
        out_shape=[field] * 3
        + [
            jax.ShapeDtypeStruct((rows // SPACING, LANES), F32),
            jax.ShapeDtypeStruct((3, 2, 2, SUB, LANES), F32),
        ],
        in_specs=[VMEM] * 8 + [ANY] * 3,
        out_specs=[ANY] * 3 + [VMEM] * 2,
        scratch_shapes=[pltpu.VMEM((tiles, 2 * STRIP + 2 * SUB, LANES), F32)] * 5
        + [pltpu.SemaphoreType.DMA((1,))],
        cost_estimate=pl.CostEstimate(flops=20 * rows * cols, bytes_accessed=16 * rows * cols, transcendentals=0),
        compiler_params=PARAMS,
        name="strips",
    )(s, e, n, d, m, ra, rb, u, si, ei, ni)


def column_kernel(
    rc, rd, own, v, si, ei, ni, xs, active, so_in, eo_in, no_in, so, eo, no, grad, S, E, N, Q, W, X, A, sem, osem
):
    del so_in, eo_in, no_in
    rows, cols = so.shape
    height = rows + 2 * HALO
    refs = (S, E, N, Q, W)
    even = is_even("lon")
    fetch = pltpu.make_async_copy(active, A, sem.at[0])
    fetch.start()
    zero_borders((S, N), height, 1)
    group = lax.div(lane_index(), HALO)

    def unpack(r):
        at = pl.ds(r - SUB, SUB)
        c, d = rc[at, :], rd[at, :]
        right, left = jnp.where(even, c, d), jnp.where(even, d, c)
        for f, dst in enumerate((S, E, N, Q)):
            a, b = right, left
            if f:
                a, b = pltpu.roll(a, LANES - f * HALO, 1), pltpu.roll(b, LANES - f * HALO, 1)
            tile = jnp.where(group == 2, a, jnp.where(group == 3, b, own[f, at, :]))
            dst[0, pl.ds(r, SUB), :] = tile
            if f == 3:
                W[0, pl.ds(r, SUB), :] = jnp.where(tile > 0.0, COURANT, 0.0)

    loop_rows(height // SUB, unpack, 40)
    lane = lane_index()
    sends = []

    def merge(fields):
        def body(r, i=None):
            at = pl.ds(r - SUB, SUB)
            for f in fields:
                tile = (S, E, N)[f][0, pl.ds(r + HALO, SUB), :]
                xi, tiles = (si, ei, ni)[f], cols // LANES
                first, last = (
                    xi[end * (tiles - 1), pl.ds(r, SUB), :] if i is None else xs[f, end, i] for end in range(2)
                )
                X[f, 0, at, :] = jnp.where(lane < EDGE, tile, first)
                X[f, 1, at, :] = jnp.where(lane >= LANES - EDGE, pltpu.roll(tile, LANES // 2, 1), last)

        loop_rows(rows // SUB, body, 32)
        body(SUB, 0)
        body(rows, 1)
        for f in fields:
            for end, col in enumerate((0, cols - LANES)):
                copy = pltpu.make_async_copy(X.at[f, end], (so, eo, no)[f].at[:, col : col + LANES], osem.at[f, end])
                copy.start()
                sends.append(copy)

    for step in range(STEPS):
        loop_rows(height // SUB, lambda r: flux_rows(refs, r, 1), 40)
        if step == STEPS - 1:
            merge((1, 2))
        loop_rows(height // SUB, lambda r: surface_rows(refs, r, 1, step == 0), 40)
    merge((0,))
    points, across = grad.shape
    cell = lax.broadcasted_iota(jnp.int32, (points, height), 1) - HALO
    table = spline_of(cell, lax.broadcasted_iota(jnp.int32, (points, height), 0))
    part = dot(table, S[0, SUB : SUB + height, :])
    index = lax.broadcasted_iota(jnp.int32, (LANES, across), 0)
    col = jnp.where(index < HALO, index, jnp.where(index < 3 * HALO, index + (cols - 2 * HALO), index - LANES))
    weights = spline_of(col, lax.broadcasted_iota(jnp.int32, (LANES, across), 1))
    weights = jnp.where((col < EDGE) | (col >= cols - EDGE), weights, 0.0)
    sums = v[:, 0:across] + dot(part, weights)
    fetch.wait()
    grad[...] = sums * A[...].astype(F32) / SPACING
    wait_all(sends)


def columns(rc, rd, own, v, si, ei, ni, xs, active, so, eo, no):
    rows, cols = so.shape
    height = rows + 2 * HALO
    field = jax.ShapeDtypeStruct((rows, cols), F32)
    return pl.pallas_call(
        column_kernel,
        out_shape=[field] * 3 + [jax.ShapeDtypeStruct(active.shape, F32)],
        in_specs=[VMEM] * 8 + [ANY] * 4,
        out_specs=[ANY] * 3 + [VMEM],
        scratch_shapes=[pltpu.VMEM((1, height + 2 * SUB, LANES), F32)] * 5
        + [
            pltpu.VMEM((3, 2, rows, LANES), F32),
            pltpu.VMEM(active.shape, jnp.int32),
            pltpu.SemaphoreType.DMA((1,)),
            pltpu.SemaphoreType.DMA((3, 2)),
        ],
        input_output_aliases={9: 0, 10: 1, 11: 2},
        compiler_params=PARAMS,
        name="columns",
    )(rc, rd, own, v, si, ei, ni, xs, in_hbm(active), so, eo, no)


def swap(array, axis, offset):
    size = lax.axis_size(axis)
    pairs = []
    for i in range(offset, size):
        j = ((i - offset) ^ 1) + offset
        if j < size:
            pairs.append((i, j))
    return lax.ppermute(array, axis, pairs)


def local(surface_adjoint, east_adjoint, north_adjoint, water_depth, wet_mask, control_active):
    fields = (surface_adjoint, east_adjoint, north_adjoint, water_depth, wet_mask)
    pa, pbc = pack_first(*fields)
    ra = swap(pa, "lat", 0)
    rbc = swap(pbc, "lat", 1)
    pb, pc, pd, own = edges(*fields)
    rb = swap(pb, "lat", 1)
    pc, pd, own = corners(ra, rbc, pc, pd, own)
    rc = swap(pc, "lon", 0)
    rd = swap(pd, "lon", 1)
    si, ei, ni, u = interior(*fields)
    so, eo, no, v, xs = strips(*fields, ra, rb, u, si, ei, ni)
    return columns(rc, rd, own, v, si, ei, ni, xs, control_active, so, eo, no)


def solution(mesh):
    spec = P("lat", "lon")
    return jax.shard_map(
        lambda *args: tuple(local(*args)),
        mesh=mesh,
        in_specs=(spec,) * 6,
        out_specs=(spec,) * 4,
        check_vma=False,
    )
```

```python
import jax
import jax.numpy as jnp
from jax import lax
from jax.experimental import pallas as pl
from jax.experimental.pallas import tpu as pltpu
from jax.sharding import PartitionSpec as P

SPACING = 16
STEPS = 3
COURANT = 0.5
LANES = 128
SUB = 8
HALO = 32
EDGE = 2 * STEPS
STRIP = HALO + 16
CHUNK = 64
F32 = jnp.float32
ANY = pl.BlockSpec(memory_space=pl.ANY)
HBM = pl.BlockSpec(memory_space=pltpu.HBM)
VMEM = pl.BlockSpec(memory_space=pltpu.VMEM)
PARAMS = pltpu.CompilerParams(vmem_limit_bytes=16 * 2**20)


def lane_index():
    return lax.broadcasted_iota(jnp.int32, (SUB, LANES), 1)


def east_minus_west(tiles):
    n = len(tiles)
    up = [pltpu.roll(t, LANES - 1, 1) for t in tiles]
    down = [pltpu.roll(t, 1, 1) for t in tiles]
    if n == 1:
        return [up[0] - down[0]]
    lane = lane_index()
    return [
        jnp.where(lane == LANES - 1, up[(c + 1) % n], up[c])
        - jnp.where(lane == 0, down[(c - 1) % n], down[c])
        for c in range(n)
    ]


def rows_at(ref, c, r):
    return ref[c, pl.ds(r, SUB), :]


def flux_rows(refs, r, tiles):
    S, E, N, Q, _ = refs
    ds = east_minus_west([rows_at(S, c, r) for c in range(tiles)])
    for c in range(tiles):
        q = rows_at(Q, c, r)
        E[c, pl.ds(r, SUB), :] = rows_at(E, c, r) + q * ds[c]
        N[c, pl.ds(r, SUB), :] = rows_at(N, c, r) + q * (rows_at(S, c, r + 1) - rows_at(S, c, r - 1))


def surface_rows(refs, r, tiles, first):
    S, E, N, _, W = refs
    de = east_minus_west([rows_at(E, c, r) for c in range(tiles)])
    for c in range(tiles):
        hw = rows_at(W, c, r)
        s = rows_at(S, c, r)
        if first:
            s = s * (hw + hw)
        S[c, pl.ds(r, SUB), :] = s + hw * (de[c] + (rows_at(N, c, r + 1) - rows_at(N, c, r - 1)))


def loop_rows(count, body, unroll=64):
    if unroll >= count:
        for i in range(count):
            body(SUB + i * SUB)
        return
    while count % unroll:
        unroll -= 1

    def step(i, carry):
        base = pl.multiple_of(i * (unroll * SUB), unroll * SUB) + SUB
        for u in range(unroll):
            body(base + u * SUB)
        return carry

    lax.fori_loop(0, count // unroll, step, 0)


def spline_weight(arg):
    mag = jnp.abs(arg)
    inner = 2.0 / 3.0 - mag * mag + 0.5 * mag * mag * mag
    outer = (2.0 - mag) * (2.0 - mag) * (2.0 - mag) / 6.0
    return jnp.where(mag < 1.0, inner, jnp.where(mag < 2.0, outer, 0.0 * mag))


def spline_of(cell, point):
    return spline_weight((cell.astype(F32) + 0.5) / SPACING - (point.astype(F32) + 0.5))


def dot(a, b):
    return jnp.dot(a, b, precision=lax.Precision.HIGHEST, preferred_element_type=F32)


def zero_borders(refs, rows, tiles):
    z = jnp.zeros((SUB, LANES), F32)
    for ref in refs:
        for c in range(tiles):
            ref[c, 0:SUB, :] = z
            ref[c, SUB + rows : SUB + rows + SUB, :] = z


def wait_all(copies):
    for copy in copies:
        copy.wait()


def is_even(axis):
    return lax.rem(lax.axis_index(axis), 2) == 0


def own_columns(first, last):
    lane = lane_index()
    both = jnp.where(lane < HALO, first, pltpu.roll(last, LANES // 2, 1))
    return jnp.where(lane < 2 * HALO, both, 0.0)


def masked(s, e, n, d, wet):
    return s, e * wet, n * wet, d * (COURANT * wet)


def pack_first_kernel(s, e, n, d, m, pa, pc, depth, mask, C, M, sem):
    rows, cols = s.shape
    even = is_even("lat")
    top = rows - HALO
    near, far = jnp.where(even, top, 0), jnp.where(even, 0, top)
    far = pl.ds(pl.multiple_of(far, SUB), HALO)
    near = pl.ds(pl.multiple_of(near, SUB), HALO)
    copies = []
    for f, src in enumerate((s, e, n, d, m)):
        for end, col in enumerate((0, cols - LANES)):
            dst = M.at[end] if f == 4 else C.at[f, end]
            copies.append(pltpu.make_async_copy(src.at[far, col : col + LANES], dst, sem.at[0]))
    for src, dst in (
        (s, pa.at[0:HALO]),
        (e, pa.at[HALO : 2 * HALO]),
        (n, pa.at[2 * HALO : 3 * HALO]),
        (d, depth),
        (m, mask),
    ):
        copies.append(pltpu.make_async_copy(src.at[near, :], dst, sem.at[1]))
    for copy in copies:
        copy.start()
    wait_all(copies[:10])
    for r in range(0, HALO, SUB):
        ends = [
            masked(*(C[f, end, r : r + SUB, :] for f in range(4)), M[end, r : r + SUB, :].astype(F32))
            for end in range(2)
        ]
        mine = [own_columns(a, b) for a, b in zip(*ends)]
        for half in range(2):
            pair = mine[2 * half] + pltpu.roll(mine[2 * half + 1], LANES // 2, 1)
            pc[half * HALO + r : half * HALO + r + SUB, :] = pair
    wait_all(copies[10:])
    wet = mask[...].astype(F32)
    pa[HALO : 2 * HALO] = pa[HALO : 2 * HALO] * wet
    pa[2 * HALO : 3 * HALO] = pa[2 * HALO : 3 * HALO] * wet
    pa[3 * HALO : 4 * HALO] = depth[...] * (COURANT * wet)


def pack_first(s, e, n, d, m):
    _, cols = s.shape
    return pl.pallas_call(
        pack_first_kernel,
        out_shape=[jax.ShapeDtypeStruct((4 * HALO, cols), F32), jax.ShapeDtypeStruct((2 * HALO, LANES), F32)],
        in_specs=[ANY] * 5,
        out_specs=[VMEM] * 2,
        scratch_shapes=[
            pltpu.VMEM((HALO, cols), F32),
            pltpu.VMEM((HALO, cols), jnp.int32),
            pltpu.VMEM((4, 2, HALO, LANES), F32),
            pltpu.VMEM((2, HALO, LANES), jnp.int32),
            pltpu.SemaphoreType.DMA((2,)),
        ],
        compiler_params=PARAMS,
        name="pack_first",
    )(*(in_hbm(x) for x in (s, e, n, d, m)))


def in_hbm(x):
    return pltpu.with_memory_space_constraint(x, pltpu.HBM)


def pack_columns(own, even):
    group = lax.div(lane_index(), HALO)
    shift = jnp.where(even, 1, 0)
    pc = pd = None
    for f, tile in enumerate(own):
        turn = (f + 2) % 4
        moved = pltpu.roll(tile, turn * HALO, 1) if turn else tile
        if pc is None:
            pc = pd = moved
        else:
            pc = jnp.where(group == lax.rem(turn + shift, 4), moved, pc)
            pd = jnp.where(group == lax.rem(turn + 1 - shift, 4), moved, pd)
    return pc, pd


def edge_kernel(s, e, n, d, m, pb, pc, pd, own, PC, PD, OWN, sem):
    rows, cols = s.shape
    lat_even, lon_even = is_even("lat"), is_even("lon")
    far = pl.multiple_of(jnp.where(lat_even, 0, rows - HALO), SUB)
    for r in range(0, HALO, SUB):
        at = pl.ds(far + r, SUB)
        wet = m[at, :].astype(F32)
        for f, value in enumerate(masked(s[at, :], e[at, :], n[at, :], d[at, :], wet)):
            pb[f * HALO + r : f * HALO + r + SUB, :] = value

    def pack(r):
        at = pl.ds(r - SUB, SUB)
        ends = []
        for col in (0, cols - LANES):
            to = slice(col, col + LANES)
            ends.append(masked(s[at, to], e[at, to], n[at, to], d[at, to], m[at, to].astype(F32)))
        mine = [own_columns(a, b) for a, b in zip(*ends)]
        for f in range(4):
            OWN[f, at, :] = mine[f]
        PC[at, :], PD[at, :] = pack_columns(mine, lon_even)

    loop_rows(rows // SUB, pack, 8)
    sends = [
        pltpu.make_async_copy(PC, pc.at[HALO : HALO + rows], sem.at[0]),
        pltpu.make_async_copy(PD, pd.at[HALO : HALO + rows], sem.at[1]),
        pltpu.make_async_copy(OWN, own.at[:, HALO : HALO + rows], sem.at[2]),
    ]
    for copy in sends:
        copy.start()
    wait_all(sends)


def edges(s, e, n, d, m):
    rows, cols = s.shape
    wide = jax.ShapeDtypeStruct((rows + 2 * HALO, LANES), F32)
    return pl.pallas_call(
        edge_kernel,
        out_shape=[
            jax.ShapeDtypeStruct((4 * HALO, cols), F32),
            wide,
            wide,
            jax.ShapeDtypeStruct((4, rows + 2 * HALO, LANES), F32),
        ],
        in_specs=[VMEM] * 5,
        out_specs=[VMEM] + [ANY] * 3,
        scratch_shapes=[
            pltpu.VMEM((rows, LANES), F32),
            pltpu.VMEM((rows, LANES), F32),
            pltpu.VMEM((4, rows, LANES), F32),
            pltpu.SemaphoreType.DMA((3,)),
        ],
        compiler_params=PARAMS,
        name="edges",
    )(s, e, n, d, m)


def corner_kernel(ra, rbc, pc_in, pd_in, own_in, pc, pd, own, PC, PD, OWN, sem):
    del pc_in, pd_in, own_in
    height = pc.shape[0]
    cols = ra.shape[1]
    even, lon_even = is_even("lat"), is_even("lon")
    top = height - HALO
    starts = (jnp.where(even, top, 0), jnp.where(even, 0, top))
    sends = []
    lane = lane_index()
    for side, row in enumerate(starts):
        for r in range(0, HALO, SUB):
            if side == 0:
                mine = [
                    own_columns(
                        ra[f * HALO + r : f * HALO + r + SUB, 0:LANES],
                        ra[f * HALO + r : f * HALO + r + SUB, cols - LANES : cols],
                    )
                    for f in range(4)
                ]
            else:
                mine = []
                for half in range(2):
                    pair = rbc[half * HALO + r : half * HALO + r + SUB, :]
                    for tile in (pair, pltpu.roll(pair, LANES // 2, 1)):
                        mine.append(jnp.where(lane < 2 * HALO, tile, 0.0))
            for f in range(4):
                OWN[side, f, r : r + SUB, :] = mine[f]
            PC[side, r : r + SUB, :], PD[side, r : r + SUB, :] = pack_columns(mine, lon_even)
        at = pl.ds(pl.multiple_of(row, SUB), HALO)
        for f, (src, dst) in enumerate(
            ((PC.at[side], pc.at[at, :]), (PD.at[side], pd.at[at, :]), (OWN.at[side], own.at[:, at, :]))
        ):
            copy = pltpu.make_async_copy(src, dst, sem.at[side, f])
            copy.start()
            sends.append(copy)
    wait_all(sends)


def corners(ra, rbc, pc, pd, own):
    return pl.pallas_call(
        corner_kernel,
        out_shape=[jax.ShapeDtypeStruct(x.shape, F32) for x in (pc, pd, own)],
        in_specs=[VMEM] * 2 + [ANY] * 3,
        out_specs=[ANY] * 3,
        scratch_shapes=[
            pltpu.VMEM((2, HALO, LANES), F32),
            pltpu.VMEM((2, HALO, LANES), F32),
            pltpu.VMEM((2, 4, HALO, LANES), F32),
            pltpu.SemaphoreType.DMA((2, 3)),
        ],
        input_output_aliases={2: 0, 3: 1, 4: 2},
        compiler_params=PARAMS,
        name="corners",
    )(ra, rbc, pc, pd, own)


def interior_kernel(s, e, n, d, m, S, E, N, u, Q, W, isem):
    rows, cols = e.shape
    tiles = cols // LANES
    chunks = rows // CHUNK
    refs = (S, E, N, Q, W)
    loads = []
    for k in range(chunks):
        loads.append([])
        for c in range(tiles):
            copy = pltpu.make_async_copy(
                s.at[k * CHUNK : (k + 1) * CHUNK, c * LANES : (c + 1) * LANES],
                S.at[c, SUB + k * CHUNK : SUB + (k + 1) * CHUNK, :],
                isem.at[k],
            )
            copy.start()
            loads[-1].append(copy)
    zero_borders((S, N), rows, tiles)

    def first_flux(r):
        ds = east_minus_west([rows_at(S, c, r) for c in range(tiles)])
        at = pl.ds(r - SUB, SUB)
        for c in range(tiles):
            to = slice(c * LANES, (c + 1) * LANES)
            wet = m[at, to].astype(F32)
            hw = COURANT * wet
            q = d[at, to] * hw
            W[c, pl.ds(r, SUB), :] = hw
            Q[c, pl.ds(r, SUB), :] = q
            E[c, pl.ds(r, SUB), :] = e[at, to] * wet + q * ds[c]
            N[c, pl.ds(r, SUB), :] = n[at, to] * wet + q * (rows_at(S, c, r + 1) - rows_at(S, c, r - 1))

    def over_chunk(k, body):
        def shifted(r):
            body(pl.multiple_of(r + k * CHUNK, SUB))

        loop_rows(CHUNK // SUB, shifted)

    wait_all(loads[0])
    for k in range(chunks):
        if k + 1 < chunks:
            wait_all(loads[k + 1])
        over_chunk(k, first_flux)
    loop_rows(rows // SUB, lambda r: surface_rows(refs, r, tiles, True))
    for _ in range(1, STEPS):
        loop_rows(rows // SUB, lambda r: flux_rows(refs, r, tiles))
        loop_rows(rows // SUB, lambda r: surface_rows(refs, r, tiles, False))
    points = rows // SPACING
    cell = lax.broadcasted_iota(jnp.int32, (points, rows), 1)
    table = spline_of(cell, lax.broadcasted_iota(jnp.int32, (points, rows), 0))
    table = jnp.where((cell >= EDGE) & (cell < rows - EDGE), table, 0.0)
    for c in range(tiles):
        u[:, c * LANES : (c + 1) * LANES] = dot(table, S[c, SUB : SUB + rows, :])


def interior(s, e, n, d, m):
    rows, cols = s.shape
    tiles = cols // LANES
    field = (tiles, rows + 2 * SUB, LANES)
    return pl.pallas_call(
        interior_kernel,
        out_shape=[jax.ShapeDtypeStruct(field, F32)] * 3 + [jax.ShapeDtypeStruct((rows // SPACING, cols), F32)],
        in_specs=[ANY] + [VMEM] * 4,
        out_specs=[VMEM] * 4,
        scratch_shapes=[pltpu.VMEM(field, F32)] * 2 + [pltpu.SemaphoreType.DMA((rows // CHUNK,))],
        cost_estimate=pl.CostEstimate(flops=40 * rows * cols, bytes_accessed=32 * rows * cols, transcendentals=0),
        compiler_params=PARAMS,
        name="interior",
    )(s, e, n, d, m)


def strip_kernel(s, e, n, d, m, ra, rb, u, si, ei, ni, so, eo, no, v, x, S, E, N, Q, W, osem):
    rows, cols = s.shape
    tiles = cols // LANES
    refs = (S, E, N, Q, W)
    even = is_even("lat")
    keep = STRIP - HALO
    count = 2 * STRIP
    sends = []
    for src, dst in ((ei, eo), (ni, no), (si, so)):
        for c in range(1, tiles - 1):
            copy = pltpu.make_async_copy(
                src.at[c, 2 * SUB : rows, :], dst.at[SUB : rows - SUB, c * LANES : (c + 1) * LANES], osem.at[0]
            )
            copy.start()
            sends.append(copy)
    zero_borders((S, N), count, tiles)
    for row, to in ((0, SUB + HALO), (rows - keep, SUB + STRIP)):
        for r in range(0, keep, SUB):
            for c in range(tiles):
                at, lanes = slice(row + r, row + r + SUB), slice(c * LANES, (c + 1) * LANES)
                wet = m[at, lanes].astype(F32)
                hw = COURANT * wet
                here = slice(to + r, to + r + SUB)
                S[c, here, :] = s[at, lanes]
                E[c, here, :] = e[at, lanes] * wet
                N[c, here, :] = n[at, lanes] * wet
                Q[c, here, :] = d[at, lanes] * hw
                W[c, here, :] = hw
    high = SUB + STRIP + keep
    for src, to in ((ra, jnp.where(even, high, SUB)), (rb, jnp.where(even, SUB, high))):
        for r in range(0, HALO, SUB):
            here = pl.ds(pl.multiple_of(to + r, SUB), SUB)
            for c in range(tiles):
                for f, dst in enumerate((S, E, N, Q)):
                    value = src[f * HALO + r : f * HALO + r + SUB, c * LANES : (c + 1) * LANES]
                    dst[c, here, :] = value
                W[c, here, :] = jnp.where(value > 0.0, COURANT, 0.0)
    for step in range(STEPS):
        loop_rows(count // SUB, lambda r: flux_rows(refs, r, tiles), 12)
        loop_rows(count // SUB, lambda r: surface_rows(refs, r, tiles, step == 0), 12)
    for f, (src, dst) in enumerate(((S, so), (E, eo), (N, no))):
        for side, (frm, to) in enumerate(((SUB + HALO, 0), (SUB + STRIP + keep - SUB, rows - SUB))):
            for c in range(tiles):
                if c in (0, tiles - 1):
                    x[f, min(c, 1), side] = src[c, frm : frm + SUB, :]
                    continue
                copy = pltpu.make_async_copy(
                    src.at[c, frm : frm + SUB, :],
                    dst.at[to : to + SUB, c * LANES : (c + 1) * LANES],
                    osem.at[0],
                )
                copy.start()
                sends.append(copy)
    points = rows // SPACING
    index = lax.broadcasted_iota(jnp.int32, (points, count), 1)
    cell = jnp.where(index < STRIP, index - HALO, index + (rows - keep - STRIP))
    table = spline_of(cell, lax.broadcasted_iota(jnp.int32, (points, count), 0))
    table = jnp.where((cell < EDGE) | (cell >= rows - EDGE), table, 0.0)
    lane = lax.broadcasted_iota(jnp.int32, (points, LANES), 1)
    parts = []
    for c in range(tiles):
        part = u[:, c * LANES : (c + 1) * LANES] + dot(table, S[c, SUB : SUB + count, :])
        if c == 0:
            part = jnp.where(lane < EDGE, 0.0, part)
        if c == tiles - 1:
            part = jnp.where(lane >= LANES - EDGE, 0.0, part)
        parts.append(part)
    weights = spline_of(
        lax.broadcasted_iota(jnp.int32, (LANES, LANES), 0),
        lax.broadcasted_iota(jnp.int32, (LANES, LANES), 1) - 2,
    )
    product = dot(jnp.concatenate(parts, axis=0), weights)
    total = jnp.zeros((points, LANES), F32)
    reach = LANES // SPACING + 4
    for c in range(tiles):
        piece = jnp.where(lane < reach, product[c * points : (c + 1) * points], 0.0)
        total = total + pltpu.roll(piece, (c * (LANES // SPACING) - 2) % LANES, 1)
    v[...] = total
    wait_all(sends)


def strips(s, e, n, d, m, ra, rb, u, si, ei, ni):
    rows, cols = s.shape
    tiles = cols // LANES
    field = jax.ShapeDtypeStruct((rows, cols), F32)
    return pl.pallas_call(
        strip_kernel,
        out_shape=[field] * 3
        + [
            jax.ShapeDtypeStruct((rows // SPACING, LANES), F32),
            jax.ShapeDtypeStruct((3, 2, 2, SUB, LANES), F32),
        ],
        in_specs=[VMEM] * 8 + [ANY] * 3,
        out_specs=[ANY] * 3 + [VMEM] * 2,
        scratch_shapes=[pltpu.VMEM((tiles, 2 * STRIP + 2 * SUB, LANES), F32)] * 5
        + [pltpu.SemaphoreType.DMA((1,))],
        cost_estimate=pl.CostEstimate(flops=20 * rows * cols, bytes_accessed=16 * rows * cols, transcendentals=0),
        compiler_params=PARAMS,
        name="strips",
    )(s, e, n, d, m, ra, rb, u, si, ei, ni)


def column_kernel(
    rc, rd, own, v, si, ei, ni, xs, active, so_in, eo_in, no_in, so, eo, no, grad, S, E, N, Q, W, X, A, sem, osem
):
    del so_in, eo_in, no_in
    rows, cols = so.shape
    height = rows + 2 * HALO
    refs = (S, E, N, Q, W)
    even = is_even("lon")
    fetch = pltpu.make_async_copy(active, A, sem.at[0])
    fetch.start()
    zero_borders((S, N), height, 1)
    group = lax.div(lane_index(), HALO)

    def unpack(r):
        at = pl.ds(r - SUB, SUB)
        c, d = rc[at, :], rd[at, :]
        right, left = jnp.where(even, c, d), jnp.where(even, d, c)
        for f, dst in enumerate((S, E, N, Q)):
            a, b = right, left
            if f:
                a, b = pltpu.roll(a, LANES - f * HALO, 1), pltpu.roll(b, LANES - f * HALO, 1)
            tile = jnp.where(group == 2, a, jnp.where(group == 3, b, own[f, at, :]))
            dst[0, pl.ds(r, SUB), :] = tile
            if f == 3:
                W[0, pl.ds(r, SUB), :] = jnp.where(tile > 0.0, COURANT, 0.0)

    loop_rows(height // SUB, unpack, 40)
    lane = lane_index()
    sends = []

    def merge(fields):
        def body(r, i=None):
            at = pl.ds(r - SUB, SUB)
            for f in fields:
                tile = (S, E, N)[f][0, pl.ds(r + HALO, SUB), :]
                xi, tiles = (si, ei, ni)[f], cols // LANES
                first, last = (
                    xi[end * (tiles - 1), pl.ds(r, SUB), :] if i is None else xs[f, end, i] for end in range(2)
                )
                X[f, 0, at, :] = jnp.where(lane < EDGE, tile, first)
                X[f, 1, at, :] = jnp.where(lane >= LANES - EDGE, pltpu.roll(tile, LANES // 2, 1), last)

        loop_rows(rows // SUB, body, 32)
        body(SUB, 0)
        body(rows, 1)
        for f in fields:
            for end, col in enumerate((0, cols - LANES)):
                copy = pltpu.make_async_copy(X.at[f, end], (so, eo, no)[f].at[:, col : col + LANES], osem.at[f, end])
                copy.start()
                sends.append(copy)

    for step in range(STEPS):
        loop_rows(height // SUB, lambda r: flux_rows(refs, r, 1), 40)
        if step == STEPS - 1:
            merge((1, 2))
        loop_rows(height // SUB, lambda r: surface_rows(refs, r, 1, step == 0), 40)
    merge((0,))
    points, across = grad.shape
    cell = lax.broadcasted_iota(jnp.int32, (points, height), 1) - HALO
    table = spline_of(cell, lax.broadcasted_iota(jnp.int32, (points, height), 0))
    part = dot(table, S[0, SUB : SUB + height, :])
    index = lax.broadcasted_iota(jnp.int32, (LANES, across), 0)
    col = jnp.where(index < HALO, index, jnp.where(index < 3 * HALO, index + (cols - 2 * HALO), index - LANES))
    weights = spline_of(col, lax.broadcasted_iota(jnp.int32, (LANES, across), 1))
    weights = jnp.where((col < EDGE) | (col >= cols - EDGE), weights, 0.0)
    sums = v[:, 0:across] + dot(part, weights)
    fetch.wait()
    grad[...] = sums * A[...].astype(F32) / SPACING
    wait_all(sends)


def columns(rc, rd, own, v, si, ei, ni, xs, active, so, eo, no):
    rows, cols = so.shape
    height = rows + 2 * HALO
    field = jax.ShapeDtypeStruct((rows, cols), F32)
    return pl.pallas_call(
        column_kernel,
        out_shape=[field] * 3 + [jax.ShapeDtypeStruct(active.shape, F32)],
        in_specs=[VMEM] * 8 + [ANY] * 4,
        out_specs=[ANY] * 3 + [VMEM],
        scratch_shapes=[pltpu.VMEM((1, height + 2 * SUB, LANES), F32)] * 5
        + [
            pltpu.VMEM((3, 2, rows, LANES), F32),
            pltpu.VMEM(active.shape, jnp.int32),
            pltpu.SemaphoreType.DMA((1,)),
            pltpu.SemaphoreType.DMA((3, 2)),
        ],
        input_output_aliases={9: 0, 10: 1, 11: 2},
        compiler_params=PARAMS,
        name="columns",
    )(rc, rd, own, v, si, ei, ni, xs, in_hbm(active), so, eo, no)


def swap(array, axis, offset):
    size = lax.axis_size(axis)
    pairs = []
    for i in range(offset, size):
        j = ((i - offset) ^ 1) + offset
        if j < size:
            pairs.append((i, j))
    return lax.ppermute(array, axis, pairs)


def local(surface_adjoint, east_adjoint, north_adjoint, water_depth, wet_mask, control_active):
    fields = (surface_adjoint, east_adjoint, north_adjoint, water_depth, wet_mask)
    pa, pbc = pack_first(*fields)
    ra = swap(pa, "lat", 0)
    rbc = swap(pbc, "lat", 1)
    pb, pc, pd, own = edges(*fields)
    rb = swap(pb, "lat", 1)
    pc, pd, own = corners(ra, rbc, pc, pd, own)
    rc = swap(pc, "lon", 0)
    rd = swap(pd, "lon", 1)
    si, ei, ni, u = interior(*fields)
    so, eo, no, v, xs = strips(*fields, ra, rb, u, si, ei, ni)
    return columns(rc, rd, own, v, si, ei, ni, xs, control_active, so, eo, no)


def solution(mesh):
    spec = P("lat", "lon")
    return jax.shard_map(
        lambda *args: tuple(local(*args)),
        mesh=mesh,
        in_specs=(spec,) * 6,
        out_specs=(spec,) * 4,
        check_vma=False,
    )
```

```python
import functools

import jax
import jax.numpy as jnp
from jax import lax
from jax.experimental import pallas as pl
from jax.experimental.pallas import tpu as pltpu
from jax.sharding import PartitionSpec as P

SPACING = 16
STEPS = 3
COURANT = 0.5
LANES = 128
SUB = 8
HALO = 32
EDGE = 2 * STEPS
STRIP = HALO + 16
CHUNK = 64
F32 = jnp.float32
ANY = pl.BlockSpec(memory_space=pl.ANY)
HBM = pl.BlockSpec(memory_space=pltpu.HBM)
VMEM = pl.BlockSpec(memory_space=pltpu.VMEM)
PARAMS = pltpu.CompilerParams(vmem_limit_bytes=16 * 2**20)


def lane_index():
    return lax.broadcasted_iota(jnp.int32, (SUB, LANES), 1)


def east_minus_west(tiles):
    n = len(tiles)
    up = [pltpu.roll(t, LANES - 1, 1) for t in tiles]
    down = [pltpu.roll(t, 1, 1) for t in tiles]
    if n == 1:
        return [up[0] - down[0]]
    lane = lane_index()
    return [
        jnp.where(lane == LANES - 1, up[(c + 1) % n], up[c])
        - jnp.where(lane == 0, down[(c - 1) % n], down[c])
        for c in range(n)
    ]


def rows_at(ref, c, r):
    return ref[c, pl.ds(r, SUB), :]


def flux_rows(refs, r, tiles):
    S, E, N, Q, _ = refs
    ds = east_minus_west([rows_at(S, c, r) for c in range(tiles)])
    for c in range(tiles):
        q = rows_at(Q, c, r)
        E[c, pl.ds(r, SUB), :] = rows_at(E, c, r) + q * ds[c]
        N[c, pl.ds(r, SUB), :] = rows_at(N, c, r) + q * (rows_at(S, c, r + 1) - rows_at(S, c, r - 1))


def surface_rows(refs, r, tiles, first):
    S, E, N, _, W = refs
    de = east_minus_west([rows_at(E, c, r) for c in range(tiles)])
    for c in range(tiles):
        hw = rows_at(W, c, r)
        s = rows_at(S, c, r)
        if first:
            s = s * (hw + hw)
        S[c, pl.ds(r, SUB), :] = s + hw * (de[c] + (rows_at(N, c, r + 1) - rows_at(N, c, r - 1)))


def loop_rows(count, body, unroll=64):
    if unroll >= count:
        for i in range(count):
            body(SUB + i * SUB)
        return
    while count % unroll:
        unroll -= 1

    def step(i, carry):
        base = pl.multiple_of(i * (unroll * SUB), unroll * SUB) + SUB
        for u in range(unroll):
            body(base + u * SUB)
        return carry

    lax.fori_loop(0, count // unroll, step, 0)


def spline_weight(arg):
    mag = jnp.abs(arg)
    inner = 2.0 / 3.0 - mag * mag + 0.5 * mag * mag * mag
    outer = (2.0 - mag) * (2.0 - mag) * (2.0 - mag) / 6.0
    return jnp.where(mag < 1.0, inner, jnp.where(mag < 2.0, outer, 0.0 * mag))


def spline_of(cell, point):
    return spline_weight((cell.astype(F32) + 0.5) / SPACING - (point.astype(F32) + 0.5))


def dot(a, b):
    ah, bh = a.astype(jnp.bfloat16), b.astype(jnp.bfloat16)
    al, bl = (a - ah.astype(F32)).astype(jnp.bfloat16), (b - bh.astype(F32)).astype(jnp.bfloat16)
    product = functools.partial(jnp.dot, preferred_element_type=F32)
    return product(ah, bh) + (product(ah, bl) + product(al, bh))


def zero_borders(refs, rows, tiles):
    z = jnp.zeros((SUB, LANES), F32)
    for ref in refs:
        for c in range(tiles):
            ref[c, 0:SUB, :] = z
            ref[c, SUB + rows : SUB + rows + SUB, :] = z


def wait_all(copies):
    for copy in copies:
        copy.wait()


def is_even(axis):
    return lax.rem(lax.axis_index(axis), 2) == 0


def own_columns(first, last):
    lane = lane_index()
    both = jnp.where(lane < HALO, first, pltpu.roll(last, LANES // 2, 1))
    return jnp.where(lane < 2 * HALO, both, 0.0)


def masked(s, e, n, d, wet):
    return s, e * wet, n * wet, d * (COURANT * wet)


def pack_first_kernel(s, e, n, d, m, pa, pc, depth, mask, C, M, sem):
    rows, cols = s.shape
    even = is_even("lat")
    top = rows - HALO
    near, far = jnp.where(even, top, 0), jnp.where(even, 0, top)
    far = pl.ds(pl.multiple_of(far, SUB), HALO)
    near = pl.ds(pl.multiple_of(near, SUB), HALO)
    copies = []
    for f, src in enumerate((s, e, n, d, m)):
        for end, col in enumerate((0, cols - LANES)):
            dst = M.at[end] if f == 4 else C.at[f, end]
            copies.append(pltpu.make_async_copy(src.at[far, col : col + LANES], dst, sem.at[0]))
    for src, dst in (
        (s, pa.at[0:HALO]),
        (e, pa.at[HALO : 2 * HALO]),
        (n, pa.at[2 * HALO : 3 * HALO]),
        (d, depth),
        (m, mask),
    ):
        copies.append(pltpu.make_async_copy(src.at[near, :], dst, sem.at[1]))
    for copy in copies:
        copy.start()
    wait_all(copies[:10])
    for r in range(0, HALO, SUB):
        ends = [
            masked(*(C[f, end, r : r + SUB, :] for f in range(4)), M[end, r : r + SUB, :].astype(F32))
            for end in range(2)
        ]
        mine = [own_columns(a, b) for a, b in zip(*ends)]
        for half in range(2):
            pair = mine[2 * half] + pltpu.roll(mine[2 * half + 1], LANES // 2, 1)
            pc[half * HALO + r : half * HALO + r + SUB, :] = pair
    wait_all(copies[10:])
    wet = mask[...].astype(F32)
    pa[HALO : 2 * HALO] = pa[HALO : 2 * HALO] * wet
    pa[2 * HALO : 3 * HALO] = pa[2 * HALO : 3 * HALO] * wet
    pa[3 * HALO : 4 * HALO] = depth[...] * (COURANT * wet)


def pack_first(s, e, n, d, m):
    _, cols = s.shape
    return pl.pallas_call(
        pack_first_kernel,
        out_shape=[jax.ShapeDtypeStruct((4 * HALO, cols), F32), jax.ShapeDtypeStruct((2 * HALO, LANES), F32)],
        in_specs=[ANY] * 5,
        out_specs=[VMEM] * 2,
        scratch_shapes=[
            pltpu.VMEM((HALO, cols), F32),
            pltpu.VMEM((HALO, cols), jnp.int32),
            pltpu.VMEM((4, 2, HALO, LANES), F32),
            pltpu.VMEM((2, HALO, LANES), jnp.int32),
            pltpu.SemaphoreType.DMA((2,)),
        ],
        compiler_params=PARAMS,
        name="pack_first",
    )(*(in_hbm(x) for x in (s, e, n, d, m)))


def in_hbm(x):
    return pltpu.with_memory_space_constraint(x, pltpu.HBM)


def pack_columns(own, even):
    group = lax.div(lane_index(), HALO)
    shift = jnp.where(even, 1, 0)
    pc = pd = None
    for f, tile in enumerate(own):
        turn = (f + 2) % 4
        moved = pltpu.roll(tile, turn * HALO, 1) if turn else tile
        if pc is None:
            pc = pd = moved
        else:
            pc = jnp.where(group == lax.rem(turn + shift, 4), moved, pc)
            pd = jnp.where(group == lax.rem(turn + 1 - shift, 4), moved, pd)
    return pc, pd


def edge_kernel(s, e, n, d, m, pb, own):
    rows, cols = s.shape
    far = pl.multiple_of(jnp.where(is_even("lat"), 0, rows - HALO), SUB)
    for r in range(0, HALO, SUB):
        at = pl.ds(far + r, SUB)
        wet = m[at, :].astype(F32)
        for f, value in enumerate(masked(s[at, :], e[at, :], n[at, :], d[at, :], wet)):
            pb[f * HALO + r : f * HALO + r + SUB, :] = value

    def pack(r):
        at = pl.ds(r - SUB, SUB)
        ends = []
        for col in (0, cols - LANES):
            to = slice(col, col + LANES)
            ends.append(masked(s[at, to], e[at, to], n[at, to], d[at, to], m[at, to].astype(F32)))
        for f, (a, b) in enumerate(zip(*ends)):
            own[f, at, :] = own_columns(a, b)

    loop_rows(rows // SUB, pack, 8)


def edges(s, e, n, d, m):
    rows, cols = s.shape
    return pl.pallas_call(
        edge_kernel,
        out_shape=[
            jax.ShapeDtypeStruct((4 * HALO, cols), F32),
            jax.ShapeDtypeStruct((4, rows, LANES), F32),
        ],
        in_specs=[VMEM] * 5,
        out_specs=[VMEM] * 2,
        compiler_params=PARAMS,
        name="edges",
    )(s, e, n, d, m)


def corner_kernel(ra, rbc, own, pc, pd, ends):
    rows, cols = own.shape[1], ra.shape[1]
    even, lon_even = is_even("lat"), is_even("lon")
    lane = lane_index()
    for side, above in enumerate((jnp.where(even, 1, 0), jnp.where(even, 0, 1))):
        for r in range(0, HALO, SUB):
            if side == 0:
                mine = [
                    own_columns(
                        ra[f * HALO + r : f * HALO + r + SUB, 0:LANES],
                        ra[f * HALO + r : f * HALO + r + SUB, cols - LANES : cols],
                    )
                    for f in range(4)
                ]
            else:
                mine = []
                for half in range(2):
                    pair = rbc[half * HALO + r : half * HALO + r + SUB, :]
                    for tile in (pair, pltpu.roll(pair, LANES // 2, 1)):
                        mine.append(jnp.where(lane < 2 * HALO, tile, 0.0))
            for f in range(4):
                ends[above, f, r : r + SUB, :] = mine[f]
            at = pl.ds(pl.multiple_of(above * (rows + HALO) + r, SUB), SUB)
            pc[at, :], pd[at, :] = pack_columns(mine, lon_even)

    def pack(r):
        at = pl.ds(r - SUB + HALO, SUB)
        mine = [own[f, pl.ds(r - SUB, SUB), :] for f in range(4)]
        pc[at, :], pd[at, :] = pack_columns(mine, lon_even)

    loop_rows(rows // SUB, pack, 8)


def corners(ra, rbc, own):
    rows = own.shape[1]
    wide = jax.ShapeDtypeStruct((rows + 2 * HALO, LANES), F32)
    return pl.pallas_call(
        corner_kernel,
        out_shape=[wide, wide, jax.ShapeDtypeStruct((2, 4, HALO, LANES), F32)],
        in_specs=[VMEM] * 3,
        out_specs=[VMEM] * 3,
        compiler_params=PARAMS,
        name="corners",
    )(ra, rbc, own)


def interior_kernel(s, e, n, d, m, S, E, N, u, Q, W, isem):
    rows, cols = e.shape
    tiles = cols // LANES
    chunks = rows // CHUNK
    refs = (S, E, N, Q, W)
    loads = []
    for k in range(chunks):
        loads.append([])
        for c in range(tiles):
            copy = pltpu.make_async_copy(
                s.at[k * CHUNK : (k + 1) * CHUNK, c * LANES : (c + 1) * LANES],
                S.at[c, SUB + k * CHUNK : SUB + (k + 1) * CHUNK, :],
                isem.at[k],
            )
            copy.start()
            loads[-1].append(copy)
    zero_borders((S, N), rows, tiles)

    def first_flux(r):
        ds = east_minus_west([rows_at(S, c, r) for c in range(tiles)])
        at = pl.ds(r - SUB, SUB)
        for c in range(tiles):
            to = slice(c * LANES, (c + 1) * LANES)
            wet = m[at, to].astype(F32)
            hw = COURANT * wet
            q = d[at, to] * hw
            W[c, pl.ds(r, SUB), :] = hw
            Q[c, pl.ds(r, SUB), :] = q
            E[c, pl.ds(r, SUB), :] = e[at, to] * wet + q * ds[c]
            N[c, pl.ds(r, SUB), :] = n[at, to] * wet + q * (rows_at(S, c, r + 1) - rows_at(S, c, r - 1))

    def over_chunk(k, body):
        def shifted(r):
            body(pl.multiple_of(r + k * CHUNK, SUB))

        loop_rows(CHUNK // SUB, shifted)

    wait_all(loads[0])
    for k in range(chunks):
        if k + 1 < chunks:
            wait_all(loads[k + 1])
        over_chunk(k, first_flux)
    loop_rows(rows // SUB, lambda r: surface_rows(refs, r, tiles, True))
    for _ in range(1, STEPS):
        loop_rows(rows // SUB, lambda r: flux_rows(refs, r, tiles))
        loop_rows(rows // SUB, lambda r: surface_rows(refs, r, tiles, False))
    points = rows // SPACING
    cell = lax.broadcasted_iota(jnp.int32, (points, rows), 1)
    table = spline_of(cell, lax.broadcasted_iota(jnp.int32, (points, rows), 0))
    table = jnp.where((cell >= EDGE) & (cell < rows - EDGE), table, 0.0)
    for c in range(tiles):
        u[:, c * LANES : (c + 1) * LANES] = dot(table, S[c, SUB : SUB + rows, :])


def interior(s, e, n, d, m):
    rows, cols = s.shape
    tiles = cols // LANES
    field = (tiles, rows + 2 * SUB, LANES)
    return pl.pallas_call(
        interior_kernel,
        out_shape=[jax.ShapeDtypeStruct(field, F32)] * 3 + [jax.ShapeDtypeStruct((rows // SPACING, cols), F32)],
        in_specs=[ANY] + [VMEM] * 4,
        out_specs=[VMEM] * 4,
        scratch_shapes=[pltpu.VMEM(field, F32)] * 2 + [pltpu.SemaphoreType.DMA((rows // CHUNK,))],
        cost_estimate=pl.CostEstimate(flops=40 * rows * cols, bytes_accessed=32 * rows * cols, transcendentals=0),
        compiler_params=PARAMS,
        name="interior",
    )(s, e, n, d, m)


def border_kernel(
    s, e, n, d, m, ra, rb, u, si, ei, ni, rc, rd, own, ends, active, so, eo, no, grad,
    S, E, N, Q, W, S1, E1, N1, Q1, W1, X, A, sem, osem,
):
    fetch = pltpu.make_async_copy(active, A, sem.at[0])
    fetch.start()
    rows, cols = s.shape
    tiles = cols // LANES
    refs = (S, E, N, Q, W)
    even = is_even("lat")
    keep = STRIP - HALO
    count = 2 * STRIP
    sends = []
    for src, dst in ((ei, eo), (ni, no), (si, so)):
        for c in range(1, tiles - 1):
            copy = pltpu.make_async_copy(
                src.at[c, 2 * SUB : rows, :], dst.at[SUB : rows - SUB, c * LANES : (c + 1) * LANES], osem.at[0]
            )
            copy.start()
            sends.append(copy)
    zero_borders((S, N), count, tiles)
    for row, to in ((0, SUB + HALO), (rows - keep, SUB + STRIP)):
        for r in range(0, keep, SUB):
            for c in range(tiles):
                at, lanes = slice(row + r, row + r + SUB), slice(c * LANES, (c + 1) * LANES)
                wet = m[at, lanes].astype(F32)
                hw = COURANT * wet
                here = slice(to + r, to + r + SUB)
                S[c, here, :] = s[at, lanes]
                E[c, here, :] = e[at, lanes] * wet
                N[c, here, :] = n[at, lanes] * wet
                Q[c, here, :] = d[at, lanes] * hw
                W[c, here, :] = hw
    high = SUB + STRIP + keep
    for src, to in ((ra, jnp.where(even, high, SUB)), (rb, jnp.where(even, SUB, high))):
        for r in range(0, HALO, SUB):
            here = pl.ds(pl.multiple_of(to + r, SUB), SUB)
            for c in range(tiles):
                for f, dst in enumerate((S, E, N, Q)):
                    value = src[f * HALO + r : f * HALO + r + SUB, c * LANES : (c + 1) * LANES]
                    dst[c, here, :] = value
                W[c, here, :] = jnp.where(value > 0.0, COURANT, 0.0)
    for step in range(STEPS):
        loop_rows(count // SUB, lambda r: flux_rows(refs, r, tiles), 12)
        loop_rows(count // SUB, lambda r: surface_rows(refs, r, tiles, step == 0), 12)
    for src, dst in ((S, so), (E, eo), (N, no)):
        for frm, to in ((SUB + HALO, 0), (SUB + STRIP + keep - SUB, rows - SUB)):
            for c in range(tiles):
                if c in (0, tiles - 1):
                    continue
                copy = pltpu.make_async_copy(
                    src.at[c, frm : frm + SUB, :],
                    dst.at[to : to + SUB, c * LANES : (c + 1) * LANES],
                    osem.at[0],
                )
                copy.start()
                sends.append(copy)
    points = rows // SPACING
    index = lax.broadcasted_iota(jnp.int32, (points, count), 1)
    cell = jnp.where(index < STRIP, index - HALO, index + (rows - keep - STRIP))
    table = spline_of(cell, lax.broadcasted_iota(jnp.int32, (points, count), 0))
    table = jnp.where((cell < EDGE) | (cell >= rows - EDGE), table, 0.0)
    lane = lax.broadcasted_iota(jnp.int32, (points, LANES), 1)
    parts = []
    for c in range(tiles):
        part = u[:, c * LANES : (c + 1) * LANES] + dot(table, S[c, SUB : SUB + count, :])
        if c == 0:
            part = jnp.where(lane < EDGE, 0.0, part)
        if c == tiles - 1:
            part = jnp.where(lane >= LANES - EDGE, 0.0, part)
        parts.append(part)
    weights = spline_of(
        lax.broadcasted_iota(jnp.int32, (LANES, LANES), 0),
        lax.broadcasted_iota(jnp.int32, (LANES, LANES), 1) - 2,
    )
    product = dot(jnp.concatenate(parts, axis=0), weights)
    total = jnp.zeros((points, LANES), F32)
    reach = LANES // SPACING + 4
    for c in range(tiles):
        piece = jnp.where(lane < reach, product[c * points : (c + 1) * points], 0.0)
        total = total + pltpu.roll(piece, (c * (LANES // SPACING) - 2) % LANES, 1)

    height = rows + 2 * HALO
    refs = column = (S1, E1, N1, Q1, W1)
    even = is_even("lon")
    zero_borders((S1, N1), height, 1)
    group = lax.div(lane_index(), HALO)

    def unpack(r):
        at = pl.ds(r - SUB, SUB)
        c, d = rc[at, :], rd[at, :]
        right, left = jnp.where(even, c, d), jnp.where(even, d, c)
        for f, dst in enumerate((S1, E1, N1, Q1)):
            a, b = right, left
            if f:
                a, b = pltpu.roll(a, LANES - f * HALO, 1), pltpu.roll(b, LANES - f * HALO, 1)
            t = r - SUB
            if t < HALO:
                middle = ends[0, f, t : t + SUB, :]
            elif t < HALO + rows:
                middle = own[f, t - HALO : t - HALO + SUB, :]
            else:
                middle = ends[1, f, t - HALO - rows : t - HALO - rows + SUB, :]
            tile = jnp.where(group == 2, a, jnp.where(group == 3, b, middle))
            dst[0, pl.ds(r, SUB), :] = tile
            if f == 3:
                W1[0, pl.ds(r, SUB), :] = jnp.where(tile > 0.0, COURANT, 0.0)

    loop_rows(height // SUB, unpack, height)
    lane = lane_index()

    def merge(fields):
        def body(r, i=None):
            at = pl.ds(r - SUB, SUB)
            for f in fields:
                tile = column[f][0, pl.ds(r + HALO, SUB), :]
                src, row = ((si, ei, ni)[f], r) if i is None else ((S, E, N)[f], i)
                first, last = (src[end * (tiles - 1), pl.ds(row, SUB), :] for end in range(2))
                X[f, 0, at, :] = jnp.where(lane < EDGE, tile, first)
                X[f, 1, at, :] = jnp.where(lane >= LANES - EDGE, pltpu.roll(tile, LANES // 2, 1), last)

        loop_rows(rows // SUB, body, 32)
        body(SUB, SUB + HALO)
        body(rows, SUB + STRIP + keep - SUB)
        for f in fields:
            for end, col in enumerate((0, cols - LANES)):
                copy = pltpu.make_async_copy(X.at[f, end], (so, eo, no)[f].at[:, col : col + LANES], osem.at[0])
                copy.start()
                sends.append(copy)

    for step in range(STEPS):
        loop_rows(height // SUB, lambda r: flux_rows(refs, r, 1), 40)
        if step == STEPS - 1:
            merge((1, 2))
        loop_rows(height // SUB, lambda r: surface_rows(refs, r, 1, step == 0), 40)
    merge((0,))
    points, across = grad.shape
    cell = lax.broadcasted_iota(jnp.int32, (points, height), 1) - HALO
    table = spline_of(cell, lax.broadcasted_iota(jnp.int32, (points, height), 0))
    part = dot(table, S1[0, SUB : SUB + height, :])
    index = lax.broadcasted_iota(jnp.int32, (LANES, across), 0)
    col = jnp.where(index < HALO, index, jnp.where(index < 3 * HALO, index + (cols - 2 * HALO), index - LANES))
    weights = spline_of(col, lax.broadcasted_iota(jnp.int32, (LANES, across), 1))
    weights = jnp.where((col < EDGE) | (col >= cols - EDGE), weights, 0.0)
    sums = total[:, 0:across] + dot(part, weights)
    fetch.wait()
    grad[...] = sums * A[...].astype(F32) / SPACING
    wait_all(sends)


def borders(s, e, n, d, m, ra, rb, u, si, ei, ni, rc, rd, own, ends, active):
    rows, cols = s.shape
    tiles = cols // LANES
    field = jax.ShapeDtypeStruct((rows, cols), F32)
    return pl.pallas_call(
        border_kernel,
        out_shape=[field] * 3 + [jax.ShapeDtypeStruct(active.shape, F32)],
        in_specs=[VMEM] * 15 + [ANY],
        out_specs=[ANY] * 3 + [VMEM],
        scratch_shapes=[pltpu.VMEM((tiles, 2 * STRIP + 2 * SUB, LANES), F32)] * 5
        + [pltpu.VMEM((1, rows + 2 * HALO + 2 * SUB, LANES), F32)] * 5
        + [
            pltpu.VMEM((3, 2, rows, LANES), F32),
            pltpu.VMEM(active.shape, jnp.int32),
            pltpu.SemaphoreType.DMA((1,)),
            pltpu.SemaphoreType.DMA((1,)),
        ],
        cost_estimate=pl.CostEstimate(flops=20 * rows * cols, bytes_accessed=16 * rows * cols, transcendentals=0),
        compiler_params=PARAMS,
        name="borders",
    )(s, e, n, d, m, ra, rb, u, si, ei, ni, rc, rd, own, ends, in_hbm(active))


def swap(array, axis, offset):
    size = lax.axis_size(axis)
    pairs = []
    for i in range(offset, size):
        j = ((i - offset) ^ 1) + offset
        if j < size:
            pairs.append((i, j))
    return lax.ppermute(array, axis, pairs)


def local(surface_adjoint, east_adjoint, north_adjoint, water_depth, wet_mask, control_active):
    fields = (surface_adjoint, east_adjoint, north_adjoint, water_depth, wet_mask)
    pa, pbc = pack_first(*fields)
    ra = swap(pa, "lat", 0)
    rbc = swap(pbc, "lat", 1)
    pb, own = edges(*fields)
    rb = swap(pb, "lat", 1)
    pc, pd, ends = corners(ra, rbc, own)
    rc = swap(pc, "lon", 0)
    rd = swap(pd, "lon", 1)
    si, ei, ni, u = interior(*fields)
    return borders(*fields, ra, rb, u, si, ei, ni, rc, rd, own, ends, control_active)


def solution(mesh):
    spec = P("lat", "lon")
    return jax.shard_map(
        lambda *args: tuple(local(*args)),
        mesh=mesh,
        in_specs=(spec,) * 6,
        out_specs=(spec,) * 4,
        check_vma=False,
    )
```

```python
import functools

import jax
import jax.numpy as jnp
from jax import lax
from jax.experimental import pallas as pl
from jax.experimental.pallas import tpu as pltpu
from jax.sharding import PartitionSpec as P

SPACING = 16
STEPS = 3
COURANT = 0.5
LANES = 128
SUB = 8
HALO = 32
EDGE = 2 * STEPS
STRIP = HALO + 16
CHUNK = 64
F32 = jnp.float32
ANY = pl.BlockSpec(memory_space=pl.ANY)
HBM = pl.BlockSpec(memory_space=pltpu.HBM)
VMEM = pl.BlockSpec(memory_space=pltpu.VMEM)
PARAMS = pltpu.CompilerParams(vmem_limit_bytes=16 * 2**20)


def lane_index():
    return lax.broadcasted_iota(jnp.int32, (SUB, LANES), 1)


def east_minus_west(tiles):
    n = len(tiles)
    up = [pltpu.roll(t, LANES - 1, 1) for t in tiles]
    down = [pltpu.roll(t, 1, 1) for t in tiles]
    if n == 1:
        return [up[0] - down[0]]
    lane = lane_index()
    return [
        jnp.where(lane == LANES - 1, up[(c + 1) % n], up[c])
        - jnp.where(lane == 0, down[(c - 1) % n], down[c])
        for c in range(n)
    ]


def rows_at(ref, c, r):
    return ref[c, pl.ds(r, SUB), :]


def flux_rows(refs, r, tiles):
    S, E, N, Q, _ = refs
    ds = east_minus_west([rows_at(S, c, r) for c in range(tiles)])
    for c in range(tiles):
        q = rows_at(Q, c, r)
        E[c, pl.ds(r, SUB), :] = rows_at(E, c, r) + q * ds[c]
        N[c, pl.ds(r, SUB), :] = rows_at(N, c, r) + q * (rows_at(S, c, r + 1) - rows_at(S, c, r - 1))


def surface_rows(refs, r, tiles, first):
    S, E, N, _, W = refs
    de = east_minus_west([rows_at(E, c, r) for c in range(tiles)])
    for c in range(tiles):
        hw = rows_at(W, c, r)
        s = rows_at(S, c, r)
        if first:
            s = s * (hw + hw)
        S[c, pl.ds(r, SUB), :] = s + hw * (de[c] + (rows_at(N, c, r + 1) - rows_at(N, c, r - 1)))


def turned(tiles, by):
    n, lane = len(tiles), lane_index()
    moved = [pltpu.roll(t, -by % LANES, 1) for t in tiles]
    if n == 1:
        return moved
    beyond = lane >= LANES - by if by > 0 else lane < -by
    step = 1 if by > 0 else -1
    return [jnp.where(beyond, moved[(c + step) % n], moved[c]) for c in range(n)]


def ahead_flux_rows(refs, r, tiles):
    S, E, N, Q, T, _ = refs
    here = [rows_at(S, c, r) for c in range(tiles)]
    ahead = turned(here, 2)
    for c in range(tiles):
        E[c, pl.ds(r, SUB), :] = rows_at(E, c, r) + rows_at(T, c, r) * (ahead[c] - here[c])
        north = rows_at(S, c, r + 1) - rows_at(S, c, r - 1)
        N[c, pl.ds(r, SUB), :] = rows_at(N, c, r) + rows_at(Q, c, r) * north


def ahead_surface_rows(refs, r, tiles, step):
    S, E, N, _, _, W = refs
    here = [rows_at(E, c, r) for c in range(tiles)]
    behind = turned(here, -2)
    for c in range(tiles):
        hw = rows_at(W, c, r)
        s = rows_at(S, c, r)
        if step == 0:
            s = s * (hw + hw)
        north = rows_at(N, c, r + 1) - rows_at(N, c, r - 1)
        S[c, pl.ds(r, SUB), :] = s + hw * ((here[c] - behind[c]) + north)
    if step == STEPS - 1:
        for c, value in enumerate(turned(here, -1)):
            E[c, pl.ds(r, SUB), :] = value


def loop_rows(count, body, unroll=64):
    if unroll >= count:
        for i in range(count):
            body(SUB + i * SUB)
        return
    while count % unroll:
        unroll -= 1

    def step(i, carry):
        base = pl.multiple_of(i * (unroll * SUB), unroll * SUB) + SUB
        for u in range(unroll):
            body(base + u * SUB)
        return carry

    lax.fori_loop(0, count // unroll, step, 0)


def spline_weight(arg):
    mag = jnp.abs(arg)
    inner = 2.0 / 3.0 - mag * mag + 0.5 * mag * mag * mag
    outer = (2.0 - mag) * (2.0 - mag) * (2.0 - mag) / 6.0
    return jnp.where(mag < 1.0, inner, jnp.where(mag < 2.0, outer, 0.0 * mag))


def spline_of(cell, point):
    return spline_weight((cell.astype(F32) + 0.5) / SPACING - (point.astype(F32) + 0.5))


def dot(a, b):
    ah, bh = a.astype(jnp.bfloat16), b.astype(jnp.bfloat16)
    al, bl = (a - ah.astype(F32)).astype(jnp.bfloat16), (b - bh.astype(F32)).astype(jnp.bfloat16)
    product = functools.partial(jnp.dot, preferred_element_type=F32)
    return product(ah, bh) + (product(ah, bl) + product(al, bh))


def zero_borders(refs, rows, tiles):
    z = jnp.zeros((SUB, LANES), F32)
    for ref in refs:
        for c in range(tiles):
            ref[c, 0:SUB, :] = z
            ref[c, SUB + rows : SUB + rows + SUB, :] = z


def wait_all(copies):
    for copy in copies:
        copy.wait()


def is_even(axis):
    return lax.rem(lax.axis_index(axis), 2) == 0


def own_columns(first, last):
    lane = lane_index()
    both = jnp.where(lane < HALO, first, pltpu.roll(last, LANES // 2, 1))
    return jnp.where(lane < 2 * HALO, both, 0.0)


def masked(s, e, n, d, wet):
    return s, e * wet, n * wet, d * (COURANT * wet)


def pack_first_kernel(s, e, n, d, m, pa, pc, depth, mask, C, M, sem):
    rows, cols = s.shape
    even = is_even("lat")
    top = rows - HALO
    near, far = jnp.where(even, top, 0), jnp.where(even, 0, top)
    far = pl.ds(pl.multiple_of(far, SUB), HALO)
    near = pl.ds(pl.multiple_of(near, SUB), HALO)
    copies = []
    for f, src in enumerate((s, e, n, d, m)):
        for end, col in enumerate((0, cols - LANES)):
            dst = M.at[end] if f == 4 else C.at[f, end]
            copies.append(pltpu.make_async_copy(src.at[far, col : col + LANES], dst, sem.at[0]))
    for src, dst in (
        (s, pa.at[0:HALO]),
        (e, pa.at[HALO : 2 * HALO]),
        (n, pa.at[2 * HALO : 3 * HALO]),
        (d, depth),
        (m, mask),
    ):
        copies.append(pltpu.make_async_copy(src.at[near, :], dst, sem.at[1]))
    for copy in copies:
        copy.start()
    wait_all(copies[:10])
    for r in range(0, HALO, SUB):
        ends = [
            masked(*(C[f, end, r : r + SUB, :] for f in range(4)), M[end, r : r + SUB, :].astype(F32))
            for end in range(2)
        ]
        mine = [own_columns(a, b) for a, b in zip(*ends)]
        for half in range(2):
            pair = mine[2 * half] + pltpu.roll(mine[2 * half + 1], LANES // 2, 1)
            pc[half * HALO + r : half * HALO + r + SUB, :] = pair
    wait_all(copies[10:])
    wet = mask[...].astype(F32)
    pa[HALO : 2 * HALO] = pa[HALO : 2 * HALO] * wet
    pa[2 * HALO : 3 * HALO] = pa[2 * HALO : 3 * HALO] * wet
    pa[3 * HALO : 4 * HALO] = depth[...] * (COURANT * wet)


def pack_first(s, e, n, d, m):
    _, cols = s.shape
    return pl.pallas_call(
        pack_first_kernel,
        out_shape=[jax.ShapeDtypeStruct((4 * HALO, cols), F32), jax.ShapeDtypeStruct((2 * HALO, LANES), F32)],
        in_specs=[ANY] * 5,
        out_specs=[VMEM] * 2,
        scratch_shapes=[
            pltpu.VMEM((HALO, cols), F32),
            pltpu.VMEM((HALO, cols), jnp.int32),
            pltpu.VMEM((4, 2, HALO, LANES), F32),
            pltpu.VMEM((2, HALO, LANES), jnp.int32),
            pltpu.SemaphoreType.DMA((2,)),
        ],
        compiler_params=PARAMS,
        name="pack_first",
    )(*(in_hbm(x) for x in (s, e, n, d, m)))


def in_hbm(x):
    return pltpu.with_memory_space_constraint(x, pltpu.HBM)


def pack_columns(own, even):
    group = lax.div(lane_index(), HALO)
    shift = jnp.where(even, 1, 0)
    pc = pd = None
    for f, tile in enumerate(own):
        turn = (f + 2) % 4
        moved = pltpu.roll(tile, turn * HALO, 1) if turn else tile
        if pc is None:
            pc = pd = moved
        else:
            pc = jnp.where(group == lax.rem(turn + shift, 4), moved, pc)
            pd = jnp.where(group == lax.rem(turn + 1 - shift, 4), moved, pd)
    return pc, pd


def edge_kernel(s, e, n, d, m, pb, own):
    rows, cols = s.shape
    far = pl.multiple_of(jnp.where(is_even("lat"), 0, rows - HALO), SUB)
    for r in range(0, HALO, SUB):
        at = pl.ds(far + r, SUB)
        wet = m[at, :].astype(F32)
        for f, value in enumerate(masked(s[at, :], e[at, :], n[at, :], d[at, :], wet)):
            pb[f * HALO + r : f * HALO + r + SUB, :] = value

    def pack(r):
        at = pl.ds(r - SUB, SUB)
        ends = []
        for col in (0, cols - LANES):
            to = slice(col, col + LANES)
            ends.append(masked(s[at, to], e[at, to], n[at, to], d[at, to], m[at, to].astype(F32)))
        for f, (a, b) in enumerate(zip(*ends)):
            own[f, at, :] = own_columns(a, b)

    loop_rows(rows // SUB, pack, 8)


def edges(s, e, n, d, m):
    rows, cols = s.shape
    return pl.pallas_call(
        edge_kernel,
        out_shape=[
            jax.ShapeDtypeStruct((4 * HALO, cols), F32),
            jax.ShapeDtypeStruct((4, rows, LANES), F32),
        ],
        in_specs=[VMEM] * 5,
        out_specs=[VMEM] * 2,
        compiler_params=PARAMS,
        name="edges",
    )(s, e, n, d, m)


def corner_kernel(ra, rbc, own, pc, pd, ends):
    rows, cols = own.shape[1], ra.shape[1]
    even, lon_even = is_even("lat"), is_even("lon")
    lane = lane_index()
    for side, above in enumerate((jnp.where(even, 1, 0), jnp.where(even, 0, 1))):
        for r in range(0, HALO, SUB):
            if side == 0:
                mine = [
                    own_columns(
                        ra[f * HALO + r : f * HALO + r + SUB, 0:LANES],
                        ra[f * HALO + r : f * HALO + r + SUB, cols - LANES : cols],
                    )
                    for f in range(4)
                ]
            else:
                mine = []
                for half in range(2):
                    pair = rbc[half * HALO + r : half * HALO + r + SUB, :]
                    for tile in (pair, pltpu.roll(pair, LANES // 2, 1)):
                        mine.append(jnp.where(lane < 2 * HALO, tile, 0.0))
            for f in range(4):
                ends[above, f, r : r + SUB, :] = mine[f]
            at = pl.ds(pl.multiple_of(above * (rows + HALO) + r, SUB), SUB)
            pc[at, :], pd[at, :] = pack_columns(mine, lon_even)

    def pack(r):
        at = pl.ds(r - SUB + HALO, SUB)
        mine = [own[f, pl.ds(r - SUB, SUB), :] for f in range(4)]
        pc[at, :], pd[at, :] = pack_columns(mine, lon_even)

    loop_rows(rows // SUB, pack, 8)


def corners(ra, rbc, own):
    rows = own.shape[1]
    wide = jax.ShapeDtypeStruct((rows + 2 * HALO, LANES), F32)
    return pl.pallas_call(
        corner_kernel,
        out_shape=[wide, wide, jax.ShapeDtypeStruct((2, 4, HALO, LANES), F32)],
        in_specs=[VMEM] * 3,
        out_specs=[VMEM] * 3,
        compiler_params=PARAMS,
        name="corners",
    )(ra, rbc, own)


def interior_kernel(s, e, n, d, m, S, E, N, u, Q, T, W, isem):
    rows, cols = e.shape
    tiles = cols // LANES
    chunks = rows // CHUNK
    refs = (S, E, N, Q, T, W)
    loads = []
    for k in range(chunks):
        loads.append([])
        for c in range(tiles):
            copy = pltpu.make_async_copy(
                s.at[k * CHUNK : (k + 1) * CHUNK, c * LANES : (c + 1) * LANES],
                S.at[c, SUB + k * CHUNK : SUB + (k + 1) * CHUNK, :],
                isem.at[k],
            )
            copy.start()
            loads[-1].append(copy)
    zero_borders((S, N), rows, tiles)

    def first_flux(r):
        at = pl.ds(r - SUB, SUB)
        here = [rows_at(S, c, r) for c in range(tiles)]
        ahead = turned(here, 2)
        flux, factor = [], []
        for c in range(tiles):
            to = slice(c * LANES, (c + 1) * LANES)
            wet = m[at, to].astype(F32)
            hw = COURANT * wet
            q = d[at, to] * hw
            W[c, pl.ds(r, SUB), :] = hw
            Q[c, pl.ds(r, SUB), :] = q
            north = rows_at(S, c, r + 1) - rows_at(S, c, r - 1)
            N[c, pl.ds(r, SUB), :] = n[at, to] * wet + q * north
            flux.append(e[at, to] * wet)
            factor.append(q)
        for c, (e1, q1) in enumerate(zip(turned(flux, 1), turned(factor, 1))):
            T[c, pl.ds(r, SUB), :] = q1
            E[c, pl.ds(r, SUB), :] = e1 + q1 * (ahead[c] - here[c])

    def over_chunk(k, body):
        def shifted(r):
            body(pl.multiple_of(r + k * CHUNK, SUB))

        loop_rows(CHUNK // SUB, shifted)

    wait_all(loads[0])
    for k in range(chunks):
        if k + 1 < chunks:
            wait_all(loads[k + 1])
        over_chunk(k, first_flux)
    loop_rows(rows // SUB, lambda r: ahead_surface_rows(refs, r, tiles, 0))
    for step in range(1, STEPS):
        loop_rows(rows // SUB, lambda r: ahead_flux_rows(refs, r, tiles))
        loop_rows(rows // SUB, lambda r: ahead_surface_rows(refs, r, tiles, step))
    points = rows // SPACING
    cell = lax.broadcasted_iota(jnp.int32, (points, rows), 1)
    table = spline_of(cell, lax.broadcasted_iota(jnp.int32, (points, rows), 0))
    table = jnp.where((cell >= EDGE) & (cell < rows - EDGE), table, 0.0)
    for c in range(tiles):
        u[:, c * LANES : (c + 1) * LANES] = dot(table, S[c, SUB : SUB + rows, :])


def interior(s, e, n, d, m):
    rows, cols = s.shape
    tiles = cols // LANES
    field = (tiles, rows + 2 * SUB, LANES)
    return pl.pallas_call(
        interior_kernel,
        out_shape=[jax.ShapeDtypeStruct(field, F32)] * 3 + [jax.ShapeDtypeStruct((rows // SPACING, cols), F32)],
        in_specs=[ANY] + [VMEM] * 4,
        out_specs=[VMEM] * 4,
        scratch_shapes=[pltpu.VMEM(field, F32)] * 3 + [pltpu.SemaphoreType.DMA((rows // CHUNK,))],
        cost_estimate=pl.CostEstimate(flops=40 * rows * cols, bytes_accessed=32 * rows * cols, transcendentals=0),
        compiler_params=PARAMS,
        name="interior",
    )(s, e, n, d, m)


def border_kernel(
    s, e, n, d, m, ra, rb, u, si, ei, ni, rc, rd, own, ends, active, so, eo, no, grad,
    S, E, N, Q, W, S1, E1, N1, Q1, W1, X, A, sem, osem,
):
    fetch = pltpu.make_async_copy(active, A, sem.at[0])
    fetch.start()
    rows, cols = s.shape
    tiles = cols // LANES
    refs = (S, E, N, Q, W)
    even = is_even("lat")
    keep = STRIP - HALO
    count = 2 * STRIP
    sends = []
    for src, dst in ((ei, eo), (ni, no), (si, so)):
        for c in range(1, tiles - 1):
            copy = pltpu.make_async_copy(
                src.at[c, 2 * SUB : rows, :], dst.at[SUB : rows - SUB, c * LANES : (c + 1) * LANES], osem.at[0]
            )
            copy.start()
            sends.append(copy)
    zero_borders((S, N), count, tiles)
    for row, to in ((0, SUB + HALO), (rows - keep, SUB + STRIP)):
        for r in range(0, keep, SUB):
            for c in range(tiles):
                at, lanes = slice(row + r, row + r + SUB), slice(c * LANES, (c + 1) * LANES)
                wet = m[at, lanes].astype(F32)
                hw = COURANT * wet
                here = slice(to + r, to + r + SUB)
                S[c, here, :] = s[at, lanes]
                E[c, here, :] = e[at, lanes] * wet
                N[c, here, :] = n[at, lanes] * wet
                Q[c, here, :] = d[at, lanes] * hw
                W[c, here, :] = hw
    high = SUB + STRIP + keep
    for src, to in ((ra, jnp.where(even, high, SUB)), (rb, jnp.where(even, SUB, high))):
        for r in range(0, HALO, SUB):
            here = pl.ds(pl.multiple_of(to + r, SUB), SUB)
            for c in range(tiles):
                for f, dst in enumerate((S, E, N, Q)):
                    value = src[f * HALO + r : f * HALO + r + SUB, c * LANES : (c + 1) * LANES]
                    dst[c, here, :] = value
                W[c, here, :] = jnp.where(value > 0.0, COURANT, 0.0)

    height = rows + 2 * HALO
    column = (S1, E1, N1, Q1, W1)
    lon_even = is_even("lon")
    zero_borders((S1, N1), height, 1)
    group = lax.div(lane_index(), HALO)

    def unpack(r):
        at = pl.ds(r - SUB, SUB)
        c, d = rc[at, :], rd[at, :]
        right, left = jnp.where(lon_even, c, d), jnp.where(lon_even, d, c)
        for f, dst in enumerate((S1, E1, N1, Q1)):
            a, b = right, left
            if f:
                a, b = pltpu.roll(a, LANES - f * HALO, 1), pltpu.roll(b, LANES - f * HALO, 1)
            t = r - SUB
            if t < HALO:
                middle = ends[0, f, t : t + SUB, :]
            elif t < HALO + rows:
                middle = own[f, t - HALO : t - HALO + SUB, :]
            else:
                middle = ends[1, f, t - HALO - rows : t - HALO - rows + SUB, :]
            tile = jnp.where(group == 2, a, jnp.where(group == 3, b, middle))
            dst[0, pl.ds(r, SUB), :] = tile
            if f == 3:
                W1[0, pl.ds(r, SUB), :] = jnp.where(tile > 0.0, COURANT, 0.0)

    loop_rows(height // SUB, unpack, height)
    lane = lane_index()

    def merge(fields):
        def body(r, i=None):
            at = pl.ds(r - SUB, SUB)
            for f in fields:
                tile = column[f][0, pl.ds(r + HALO, SUB), :]
                src, row = ((si, ei, ni)[f], r) if i is None else ((S, E, N)[f], i)
                first, last = (src[end * (tiles - 1), pl.ds(row, SUB), :] for end in range(2))
                X[f, 0, at, :] = jnp.where(lane < EDGE, tile, first)
                X[f, 1, at, :] = jnp.where(lane >= LANES - EDGE, pltpu.roll(tile, LANES // 2, 1), last)

        loop_rows(rows // SUB, body, 32)
        body(SUB, SUB + HALO)
        body(rows, SUB + STRIP + keep - SUB)
        for f in fields:
            for end, col in enumerate((0, cols - LANES)):
                copy = pltpu.make_async_copy(X.at[f, end], (so, eo, no)[f].at[:, col : col + LANES], osem.at[0])
                copy.start()
                sends.append(copy)

    for step in range(STEPS):
        loop_rows(count // SUB, lambda r: flux_rows(refs, r, tiles))
        loop_rows(height // SUB, lambda r: flux_rows(column, r, 1))
        if step == STEPS - 1:
            merge((1, 2))
        loop_rows(count // SUB, lambda r: surface_rows(refs, r, tiles, step == 0))
        loop_rows(height // SUB, lambda r: surface_rows(column, r, 1, step == 0))
    merge((0,))
    for src, dst in ((S, so), (E, eo), (N, no)):
        for frm, to in ((SUB + HALO, 0), (SUB + STRIP + keep - SUB, rows - SUB)):
            for c in range(tiles):
                if c in (0, tiles - 1):
                    continue
                copy = pltpu.make_async_copy(
                    src.at[c, frm : frm + SUB, :],
                    dst.at[to : to + SUB, c * LANES : (c + 1) * LANES],
                    osem.at[0],
                )
                copy.start()
                sends.append(copy)
    points = rows // SPACING
    index = lax.broadcasted_iota(jnp.int32, (points, count), 1)
    cell = jnp.where(index < STRIP, index - HALO, index + (rows - keep - STRIP))
    table = spline_of(cell, lax.broadcasted_iota(jnp.int32, (points, count), 0))
    table = jnp.where((cell < EDGE) | (cell >= rows - EDGE), table, 0.0)
    lane = lax.broadcasted_iota(jnp.int32, (points, LANES), 1)
    parts = []
    for c in range(tiles):
        part = u[:, c * LANES : (c + 1) * LANES] + dot(table, S[c, SUB : SUB + count, :])
        if c == 0:
            part = jnp.where(lane < EDGE, 0.0, part)
        if c == tiles - 1:
            part = jnp.where(lane >= LANES - EDGE, 0.0, part)
        parts.append(part)
    weights = spline_of(
        lax.broadcasted_iota(jnp.int32, (LANES, LANES), 0),
        lax.broadcasted_iota(jnp.int32, (LANES, LANES), 1) - 2,
    )
    product = dot(jnp.concatenate(parts, axis=0), weights)
    total = jnp.zeros((points, LANES), F32)
    reach = LANES // SPACING + 4
    for c in range(tiles):
        piece = jnp.where(lane < reach, product[c * points : (c + 1) * points], 0.0)
        total = total + pltpu.roll(piece, (c * (LANES // SPACING) - 2) % LANES, 1)
    points, across = grad.shape
    cell = lax.broadcasted_iota(jnp.int32, (points, height), 1) - HALO
    table = spline_of(cell, lax.broadcasted_iota(jnp.int32, (points, height), 0))
    part = dot(table, S1[0, SUB : SUB + height, :])
    index = lax.broadcasted_iota(jnp.int32, (LANES, across), 0)
    col = jnp.where(index < HALO, index, jnp.where(index < 3 * HALO, index + (cols - 2 * HALO), index - LANES))
    weights = spline_of(col, lax.broadcasted_iota(jnp.int32, (LANES, across), 1))
    weights = jnp.where((col < EDGE) | (col >= cols - EDGE), weights, 0.0)
    sums = total[:, 0:across] + dot(part, weights)
    fetch.wait()
    grad[...] = sums * A[...].astype(F32) / SPACING
    wait_all(sends)


def borders(s, e, n, d, m, ra, rb, u, si, ei, ni, rc, rd, own, ends, active):
    rows, cols = s.shape
    tiles = cols // LANES
    field = jax.ShapeDtypeStruct((rows, cols), F32)
    return pl.pallas_call(
        border_kernel,
        out_shape=[field] * 3 + [jax.ShapeDtypeStruct(active.shape, F32)],
        in_specs=[VMEM] * 15 + [ANY],
        out_specs=[ANY] * 3 + [VMEM],
        scratch_shapes=[pltpu.VMEM((tiles, 2 * STRIP + 2 * SUB, LANES), F32)] * 5
        + [pltpu.VMEM((1, rows + 2 * HALO + 2 * SUB, LANES), F32)] * 5
        + [
            pltpu.VMEM((3, 2, rows, LANES), F32),
            pltpu.VMEM(active.shape, jnp.int32),
            pltpu.SemaphoreType.DMA((1,)),
            pltpu.SemaphoreType.DMA((1,)),
        ],
        cost_estimate=pl.CostEstimate(flops=20 * rows * cols, bytes_accessed=16 * rows * cols, transcendentals=0),
        compiler_params=PARAMS,
        name="borders",
    )(s, e, n, d, m, ra, rb, u, si, ei, ni, rc, rd, own, ends, in_hbm(active))


def swap(array, axis, offset):
    size = lax.axis_size(axis)
    pairs = []
    for i in range(offset, size):
        j = ((i - offset) ^ 1) + offset
        if j < size:
            pairs.append((i, j))
    return lax.ppermute(array, axis, pairs)


def local(surface_adjoint, east_adjoint, north_adjoint, water_depth, wet_mask, control_active):
    fields = (surface_adjoint, east_adjoint, north_adjoint, water_depth, wet_mask)
    pa, pbc = pack_first(*fields)
    ra = swap(pa, "lat", 0)
    rbc = swap(pbc, "lat", 1)
    pb, own = edges(*fields)
    rb = swap(pb, "lat", 1)
    pc, pd, ends = corners(ra, rbc, own)
    rc = swap(pc, "lon", 0)
    rd = swap(pd, "lon", 1)
    si, ei, ni, u = interior(*fields)
    return borders(*fields, ra, rb, u, si, ei, ni, rc, rd, own, ends, control_active)


def solution(mesh):
    spec = P("lat", "lon")
    return jax.shard_map(
        lambda *args: tuple(local(*args)),
        mesh=mesh,
        in_specs=(spec,) * 6,
        out_specs=(spec,) * 4,
        check_vma=False,
    )
```
